32 devices in a mesh: seg: 4 (over y, x), coil: 8 (over z, core).
Axes of the slice: x: 2, y: 2, z: 4, core: 2. Of those that a mesh axis runs over, the one named last changes fastest.
Arguments:
- image_estimate: bfloat16 [1, 384, 768], replicated, may hold values from -6 to 6
- coil_maps: bfloat16 [8, 384, 768], P('coil'), may hold values from -3 to 3
- field_map: float32 [384, 384], replicated, may hold values from -3 to 3
- interp_rows: bfloat16 [1, 256, 384], replicated, may hold values from -0.3125 to 0.3125
- interp_cols: bfloat16 [1, 128, 384], replicated, may hold values from -0.3125 to 0.3125
- measured: bfloat16 [8, 1, 256, 256], P('coil'), may hold values from -6 to 6
- sample_time: int32 [1, 256], replicated, may hold values from 0 to 12
- sample_count: int32 [1], replicated, may hold values from 128 to 256
Outputs:
- gradient: float32 [1, 384, 768], P(None, 'coil', 'seg')
- residual: float32 [8, 1, 256, 256], P('coil', None, 'seg')
The draws below stay inside these ranges and needn't reach their ends.
Inputs may be any that keep to these rules, and one draw needn't show every extreme that they name: sample_time counts the sample clock, 4 steps to a segment. Rows below sample_count[p] of partition p are acquired.
All inputs are finite; a program needn't handle non-finite values.
Results may differ from the reference program's by a relative error of at most 0.017.
Values sent between devices are 32-bit elements; how exact they have to be, the bound alone decides.
No kernel may reach another device: no remote copies, remote signals or barrier semaphores. Data moves between devices by JAX's collectives and lax.ppermute only.
A program may use at most 64 MiB of HBM per device.

```python
import jax
import jax.numpy as jnp
from jax import lax

NPIX = 384
SROWS = 256
SCOLS = 128
PARTS_SIZE = 1
SUBSTEPS = 4
NSEG = 4
COILS = 8


def plant(values, own_key, low, top_value):
    longest = values.shape.index(max(values.shape))
    spots = []
    for shift in (0, 1):
        where = [jax.random.randint(jax.random.fold_in(own_key, axis), (), 0, length) for axis, length in enumerate(values.shape)]
        where[longest] = (where[longest] + shift) % values.shape[longest]
        spots.append(tuple(where))
    return values.at[spots[0]].set(low).at[spots[1]].set(top_value)


def steps_of(own_key, dims, cuts, least, top_value):
    gain, own = 1.0, jax.random.fold_in(own_key, 6)
    for dim, parts in cuts:
        heights = jnp.exp(jax.random.uniform(jax.random.fold_in(own, dim), (parts,), jnp.float32, least / len(cuts), top_value / len(cuts)))
        gain = gain * jnp.repeat(heights, dims[dim] // parts).reshape([-1 if axis == dim else 1 for axis in range(len(dims))])
    return gain


def bell_draw(key, dims, scale, bound, pieces=(), kind=jnp.bfloat16):
    values = scale * jax.random.normal(key, dims, jnp.float32)
    if pieces:
        values = values * steps_of(key, dims, pieces, -0.22, 0.18)
    return jnp.clip(values, -bound, bound).astype(kind)


def setup_inputs(seed: int = 0) -> dict:
    arg_keys = jax.random.split(jax.random.key(seed), 9)
    return {
        "image_estimate": bell_draw(arg_keys[0], (PARTS_SIZE, NPIX, 2 * NPIX), 1.0, 6.0),
        "coil_maps": bell_draw(arg_keys[1], (COILS, NPIX, 2 * NPIX), 0.5, 3.0, ((0, 8),)),
        "field_map": jnp.clip(jax.random.uniform(arg_keys[2], (NPIX, NPIX), jnp.float32, -3.0, 3.0), -3.0, 3.0),
        "interp_rows": bell_draw(arg_keys[3], (PARTS_SIZE, SROWS, NPIX), NPIX ** -0.5, 0.3125),
        "interp_cols": bell_draw(arg_keys[4], (PARTS_SIZE, SCOLS, NPIX), NPIX ** -0.5, 0.3125),
        "measured": bell_draw(arg_keys[5], (COILS, PARTS_SIZE, SROWS, 2 * SCOLS), 1.0, 6.0, ((0, 8),)),
        "sample_time": plant(jax.random.randint(arg_keys[6], (PARTS_SIZE, SROWS), 0, (NSEG - 1) * SUBSTEPS + 1), jax.random.fold_in(arg_keys[6], 1), 0, (NSEG - 1) * SUBSTEPS).astype(jnp.int32),
        "sample_count": jax.random.randint(arg_keys[7], (PARTS_SIZE,), SROWS // 2, SROWS + 1).astype(jnp.int32),
    }


def seg_weights(sample_steps, segment):
    distance = jnp.abs(sample_steps.astype(jnp.float32) - (segment * SUBSTEPS).astype(jnp.float32)) / SUBSTEPS
    return jnp.maximum(0.0, 1.0 - distance)


def to_complex(halves):
    width = halves.shape[-1] // 2
    return halves[..., :width].astype(jnp.float32) + 1j * halves[..., width:].astype(jnp.float32)


def to_halves(values):
    return jnp.concatenate([jnp.real(values), jnp.imag(values)], axis=-1)


def reference(image_estimate, coil_maps, field_map, interp_rows, interp_cols, measured, sample_time, sample_count):
    row_ids = jnp.arange(SROWS, dtype=jnp.int32)
    factor = COILS ** -0.5
    gradients = []
    residuals = []
    for part in range(PARTS_SIZE):
        current = to_complex(image_estimate[part])
        grid_rows = interp_rows[part]
        grid_cols = interp_cols[part].astype(jnp.float32)
        sample_steps = sample_time[part]
        sampled_mask = (row_ids < sample_count[part]).astype(jnp.float32)[:, None]

        def coil_step(total, inputs):
            coil_map, coil_data = inputs
            sensitivity = to_complex(coil_map)

            def phased(segment):
                angles = field_map * (segment.astype(jnp.float32) - 0.5 * (NSEG - 1))
                return sensitivity * (jnp.cos(angles) + 1j * jnp.sin(angles))

            def forward(segment, accum):
                weighted = to_halves(current * phased(segment)).astype(jnp.bfloat16)
                rows_ft = to_halves(jnp.fft.fft(to_complex(weighted), axis=0, norm="ortho")).astype(jnp.bfloat16)
                kspace = to_halves(jnp.fft.fft(to_complex(rows_ft), axis=1, norm="ortho")).astype(jnp.bfloat16)
                picked = jnp.dot(grid_rows, kspace, preferred_element_type=jnp.float32).astype(jnp.bfloat16)
                return accum + seg_weights(sample_steps, segment)[:, None] * picked.astype(jnp.float32)

            accum = lax.fori_loop(0, NSEG, forward, jnp.zeros((SROWS, 2 * NPIX), jnp.float32))
            samples = jnp.einsum("mrn,kn->mrk", accum.reshape(SROWS, 2, NPIX), grid_cols,
                                 precision=lax.Precision.HIGHEST).reshape(SROWS, 2 * SCOLS)
            misfit = sampled_mask * (samples - coil_data.astype(jnp.float32))

            def adjoint(segment, image_sum):
                back_weighted = (seg_weights(sample_steps, segment)[:, None] * misfit).astype(jnp.bfloat16)
                spread = jnp.dot(grid_rows.T, back_weighted, preferred_element_type=jnp.float32).astype(jnp.bfloat16)
                gridded = jnp.einsum("nrk,kj->nrj", spread.reshape(NPIX, 2, SCOLS).astype(jnp.float32), grid_cols,
                                     precision=lax.Precision.HIGHEST).reshape(NPIX, 2 * NPIX).astype(jnp.bfloat16)
                back_rows = to_halves(jnp.fft.ifft(to_complex(gridded), axis=0, norm="ortho")).astype(jnp.bfloat16)
                back_image = jnp.fft.ifft(to_complex(back_rows), axis=1, norm="ortho")
                return image_sum + to_halves(jnp.conj(phased(segment)) * back_image)

            coil_image = lax.fori_loop(0, NSEG, adjoint, jnp.zeros((NPIX, 2 * NPIX), jnp.float32))
            return total + coil_image, misfit

        total, misfits = lax.scan(coil_step, jnp.zeros((NPIX, 2 * NPIX), jnp.float32),
                                  (coil_maps, measured[:, part]))
        gradients.append(factor * total)
        residuals.append(misfits)
    return jnp.stack(gradients, axis=0), jnp.stack(residuals, axis=1)
```

```python
import math

import jax
import jax.numpy as jnp
import numpy as np
from jax import lax
from jax.sharding import PartitionSpec as P

SUBSTEPS = 4


def dft_tables(length):
    wrapped = np.outer(np.arange(length), np.arange(length)) % length
    angles = wrapped * (2.0 * math.pi / length)
    factor = 1.0 / math.sqrt(length)
    return np.cos(angles) * factor, -np.sin(angles) * factor


def dot(a, b):
    return jnp.dot(a, b, preferred_element_type=jnp.float32)


def exchange_sum(blocks, axis):
    total = lax.axis_size(axis)
    me = lax.axis_index(axis)
    lane = me % 2
    group = me // 2
    groups = total // 2
    split = blocks.reshape(groups, 2, *blocks.shape[1:])
    away = lax.dynamic_index_in_dim(split, 1 - lane, 1, False)
    kept = lax.dynamic_index_in_dim(split, lane, 1, False)
    paired = kept + lax.ppermute(away, axis, [(i, i ^ 1) for i in range(total)])
    result = lax.dynamic_index_in_dim(paired, group, 0, False)
    for step in range(1, groups):
        piece = lax.dynamic_index_in_dim(paired, (group + step) % groups, 0, False)
        result = result + lax.ppermute(
            piece, axis, [(i, (i + 2 * step) % total) for i in range(total)]
        )
    return result


def shards(
    image_estimate,
    coil_maps,
    field_map,
    interp_rows,
    interp_cols,
    measured,
    sample_time,
    sample_count,
):
    segment = lax.axis_index("seg")
    seg_total = lax.axis_size("seg")
    coil_total = lax.axis_size("coil")
    pixels = field_map.shape[0]
    row_total = interp_rows.shape[1]
    own_rows = row_total // seg_total
    width = 2 * pixels // seg_total
    column = (segment * width) % pixels
    imaginary = segment * width >= pixels
    fourier_re, fourier_im = dft_tables(pixels)
    fourier = jnp.asarray(np.concatenate([fourier_re, fourier_im], 1), jnp.bfloat16)
    row_op = dot(interp_rows[0], fourier).astype(jnp.bfloat16)
    col_op = dot(interp_cols[0], fourier).astype(jnp.bfloat16)
    row_re, row_im = row_op[:, :pixels], row_op[:, pixels:]
    col_re, col_im = col_op[:, :pixels], col_op[:, pixels:]
    maps = coil_maps[0].astype(jnp.float32)
    sens_re, sens_im = maps[:, :pixels], maps[:, pixels:]
    current = image_estimate[0].astype(jnp.float32)
    cur_re, cur_im = current[:, :pixels], current[:, pixels:]
    base_re = cur_re * sens_re - cur_im * sens_im
    base_im = cur_re * sens_im + cur_im * sens_re
    steps = sample_time[0].astype(jnp.float32)
    col_right = jnp.concatenate(
        [jnp.concatenate([col_re, -col_im], 1), jnp.concatenate([col_im, col_re], 1)], 0
    )
    samples = 0.0
    phases = []
    weights = []
    for s in range(seg_total):
        angles = field_map * (s - 0.5 * (seg_total - 1))
        phase_re, phase_im = jnp.cos(angles), jnp.sin(angles)
        phases.append((phase_re, phase_im))
        weight = jnp.maximum(0.0, 1.0 - jnp.abs(steps - s * SUBSTEPS) / SUBSTEPS)[:, None]
        weights.append(weight)
        weighted = jnp.concatenate(
            [base_re * phase_re - base_im * phase_im, base_re * phase_im + base_im * phase_re], 1
        ).astype(jnp.bfloat16)
        v = lax.dot_general(
            weighted, col_right, (((1,), (1,)), ((), ())), preferred_element_type=jnp.float32
        ).astype(jnp.bfloat16)
        half = v.shape[1] // 2
        turned = jnp.concatenate([-v[:, half:], v[:, :half]], 1)
        samples = samples + weight * dot(
            jnp.concatenate([row_re, row_im], 1), jnp.concatenate([v, turned], 0)
        )
    mask = (jnp.arange(row_total) < sample_count[0]).astype(jnp.float32)[:, None]
    misfit = mask * (samples - measured[0, 0].astype(jnp.float32))
    own = lax.dynamic_slice_in_dim(misfit, segment * own_rows, own_rows, 0)
    part_re = lax.dynamic_slice_in_dim(col_re, column, width, 1)
    part_im = lax.dynamic_slice_in_dim(col_im, column, width, 1)
    col_left = jnp.concatenate(
        [jnp.concatenate([part_re, -part_im], 1), jnp.concatenate([part_im, part_re], 1)], 0
    )
    turned = dot(misfit.astype(jnp.bfloat16), col_left)
    turn_re, turn_im = turned[:, :width], turned[:, width:]
    row_stack = jnp.concatenate([row_re, row_im], 0)
    sum_re = 0.0
    sum_im = 0.0
    for s in range(seg_total):
        top = jnp.concatenate([turn_re, turn_im], 1) * weights[s]
        low = jnp.concatenate([turn_im, -turn_re], 1) * weights[s]
        image = lax.dot_general(
            row_stack,
            jnp.concatenate([top, low], 0).astype(jnp.bfloat16),
            (((0,), (0,)), ((), ())),
            preferred_element_type=jnp.float32,
        )
        image_re, image_im = image[:, :width], image[:, width:]
        phase_re = lax.dynamic_slice_in_dim(phases[s][0], column, width, 1)
        phase_im = lax.dynamic_slice_in_dim(phases[s][1], column, width, 1)
        sum_re = sum_re + phase_re * image_re + phase_im * image_im
        sum_im = sum_im + phase_re * image_im - phase_im * image_re
    map_re = lax.dynamic_slice_in_dim(sens_re, column, width, 1)
    map_im = lax.dynamic_slice_in_dim(sens_im, column, width, 1)
    first = jnp.where(imaginary, -map_im, map_re)
    second = jnp.where(imaginary, map_re, map_im)
    term = coil_total ** (-0.5) * (first * sum_re + second * sum_im)
    gradient = exchange_sum(term.reshape(coil_total, pixels // coil_total, width), "coil")
    return gradient[None], own[None, None]


def solution(mesh):
    in_specs = (P(), P("coil", None, None), P(), P(), P(), P("coil", None, None, None), P(), P())
    out_specs = (P(None, "coil", "seg"), P("coil", None, "seg", None))
    return jax.shard_map(shards, mesh=mesh, in_specs=in_specs, out_specs=out_specs, check_vma=False)
```

```python
import functools
import math

import jax
import jax.numpy as jnp
import numpy as np
from jax import lax
from jax.experimental import pallas as pl
from jax.experimental.pallas import tpu as pltpu
from jax.sharding import PartitionSpec as P

SUBSTEPS = 4
LANES = 128
WINDOW = 256
CHUNK = 128


def dft_tables(length):
    wrapped = np.outer(np.arange(length), np.arange(length)) % length
    angles = wrapped * (2.0 * math.pi / length)
    factor = 1.0 / math.sqrt(length)
    return np.concatenate([np.cos(angles) * factor, -np.sin(angles) * factor], 1)


def dot(a, b, contract=((1,), (0,))):
    return lax.dot_general(a, b, (contract, ((), ())), preferred_element_type=jnp.float32)


def sine_cosine(x):
    y = x * x
    sine = -1.0 / math.factorial(11)
    for power in (9, 7, 5, 3):
        sine = sine * y + (-1.0) ** (power // 2) / math.factorial(power)
    sine = x * (sine * y + 1.0)
    cosine = 1.0 / math.factorial(12)
    for power in (10, 8, 6, 4, 2):
        cosine = cosine * y + (-1.0) ** (power // 2) / math.factorial(power)
    return sine, cosine * y + 1.0


def local_kernel(
    seg_total,
    coil_total,
    packed,
    count_ref,
    time_ref,
    rows_hbm,
    fourier_hbm,
    cols_hbm,
    field_hbm,
    maps_hbm,
    image_hbm,
    measured_hbm,
    term_ref,
    own_ref,
    rows_ref,
    fourier_ref,
    cols_ref,
    field_ref,
    maps_ref,
    image_ref,
    measured_ref,
    wave_ref,
    phase_ref,
    left_ref,
    right_ref,
    misfit_ref,
    adjoint_ref,
    turned_ref,
    sems,
):
    pixels = field_ref.shape[0]
    row_total = rows_ref.shape[0]
    col_total = cols_ref.shape[0]
    own_rows = row_total // seg_total
    width = 2 * pixels // seg_total
    pairs = seg_total // 2
    block_rows = pixels // coil_total
    segment = lax.axis_index("seg")
    member = lax.axis_index("coil")

    copies = [
        pltpu.make_async_copy(source, target, sems.at[i])
        for i, (source, target) in enumerate(
            (
                (rows_hbm, rows_ref),
                (fourier_hbm, fourier_ref),
                (cols_hbm, cols_ref),
                (field_hbm, field_ref),
                (maps_hbm, maps_ref),
                (image_hbm, image_ref),
                (measured_hbm, measured_ref),
            )
        )
    ]
    for copy in copies:
        copy.start()
    for copy in copies[:3]:
        copy.wait()

    grid_rows = rows_ref[...]
    grid_cols = cols_ref[...]
    fourier = fourier_ref[...]
    row_op = dot(grid_rows, fourier).astype(jnp.bfloat16)
    for part in range(2):
        span = slice(part * pixels, (part + 1) * pixels)
        adjoint_ref[:, part * row_total : (part + 1) * row_total] = dot(
            fourier[:, span], grid_rows, ((1,), (1,))
        ).astype(jnp.bfloat16)
    col_op = dot(grid_cols, fourier).astype(jnp.bfloat16)
    left_ref[:col_total, :pixels] = col_op[:, :pixels]
    left_ref[:col_total, pixels:] = -col_op[:, pixels:]
    left_ref[col_total:, :pixels] = col_op[:, pixels:]
    left_ref[col_total:, pixels:] = col_op[:, :pixels]
    col_re = dot(fourier[:, :pixels], grid_cols, ((1,), (1,))).astype(jnp.bfloat16)
    col_im = dot(fourier[:, pixels:], grid_cols, ((1,), (1,))).astype(jnp.bfloat16)
    right_ref[:pixels, :col_total] = col_re
    right_ref[:pixels, col_total:] = col_im
    right_ref[pixels:, :col_total] = -col_im
    right_ref[pixels:, col_total:] = col_re

    steps = jnp.broadcast_to(time_ref[...].astype(jnp.float32), (8, row_total))
    def weight(s):
        return jnp.maximum(0.0, 1.0 - jnp.abs(steps - float(s * SUBSTEPS)) / SUBSTEPS)
    along = []
    for pair in range(pairs):
        above, below = weight(pairs + pair), weight(pairs - 1 - pair)
        along += [above + below, above - below]

    for copy in copies[3:6]:
        copy.wait()
    right = right_ref[...]
    samples = None
    contracted = [[] for _ in range(seg_total)]
    for top in range(0, pixels, CHUNK):
        rows = slice(top, top + CHUNK)
        sine, cosine = sine_cosine(0.5 * field_ref[rows, :])
        image_re = image_ref[rows, :pixels].astype(jnp.float32)
        image_im = image_ref[rows, pixels:].astype(jnp.float32)
        map_re = maps_ref[rows, :pixels].astype(jnp.float32)
        map_im = maps_ref[rows, pixels:].astype(jnp.float32)
        base_re = image_re * map_re - image_im * map_im
        base_im = image_re * map_im + image_im * map_re
        twice_re = cosine * cosine - sine * sine
        twice_im = 2.0 * cosine * sine
        for pair in range(pairs):
            if pair:
                cosine, sine = (
                    cosine * twice_re - sine * twice_im,
                    cosine * twice_im + sine * twice_re,
                )
            phase_ref[2 * pair, rows, :] = cosine
            phase_ref[2 * pair + 1, rows, :] = sine
            wave_ref[2 * pair, rows, :pixels] = (base_re * cosine).astype(jnp.bfloat16)
            wave_ref[2 * pair, rows, pixels:] = (base_im * cosine).astype(jnp.bfloat16)
            wave_ref[2 * pair + 1, rows, :pixels] = (-base_im * sine).astype(jnp.bfloat16)
            wave_ref[2 * pair + 1, rows, pixels:] = (base_re * sine).astype(jnp.bfloat16)
        for i in range(seg_total):
            contracted[i].append(dot(wave_ref[i, rows, :], right).astype(jnp.bfloat16))
    for i in range(seg_total):
        v = jnp.concatenate(contracted[i], 0)
        turned = jnp.concatenate([-v[:, col_total:], v[:, :col_total]], 1)
        y = dot(row_op[:, :pixels], v) + dot(row_op[:, pixels:], turned)
        y = y * jnp.transpose(along[i])[:, :1]
        samples = y if samples is None else samples + y

    copies[6].wait()
    row_ids = lax.broadcasted_iota(jnp.int32, (row_total, 2 * col_total), 0)
    misfit = samples - measured_ref[...].astype(jnp.float32)
    misfit = jnp.where(row_ids < count_ref[0], misfit, 0.0)
    misfit_ref[...] = misfit
    own_start = pl.multiple_of(segment * own_rows, own_rows)
    own_copy = pltpu.make_async_copy(misfit_ref.at[pl.ds(own_start, own_rows)], own_ref, sems.at[7])
    own_copy.start()

    column = lax.rem(segment * width, pixels)
    imaginary = segment * width >= pixels
    start = jnp.minimum(column // LANES * LANES, pixels - WINDOW)
    start = pl.multiple_of(start, LANES)
    shift = column - start
    part_re = left_ref[:, pl.ds(start, WINDOW)]
    part_im = left_ref[:, pl.ds(pl.multiple_of(start + pixels, LANES), WINDOW)]
    misfit = misfit.astype(jnp.bfloat16)
    turn_re = dot(misfit, part_re).astype(jnp.bfloat16)
    turn_im = dot(misfit, part_im).astype(jnp.bfloat16)
    turned_ref[:row_total, :WINDOW] = turn_re
    turned_ref[:row_total, WINDOW:] = turn_im
    turned_ref[row_total:, :WINDOW] = turn_im
    turned_ref[row_total:, WINDOW:] = -turn_re
    turned = turned_ref[...]
    factor = coil_total ** (-0.5)
    for top in range(0, pixels, CHUNK):
        rows = slice(top, top + CHUNK)
        adjoint = adjoint_ref[rows, :]
        sum_re = None
        for pair in range(pairs):
            cosine = phase_ref[2 * pair, rows, pl.ds(start, WINDOW)]
            sine = phase_ref[2 * pair + 1, rows, pl.ds(start, WINDOW)]
            scale = [
                jnp.concatenate([along[2 * pair + i][:1]] * 2, 1).astype(jnp.bfloat16)
                for i in range(2)
            ]
            even = dot(adjoint * scale[0], turned)
            odd = dot(adjoint * scale[1], turned)
            add_re = cosine * even[:, :WINDOW] + sine * odd[:, WINDOW:]
            add_im = cosine * even[:, WINDOW:] - sine * odd[:, :WINDOW]
            sum_re = add_re if sum_re is None else sum_re + add_re
            sum_im = add_im if pair == 0 else sum_im + add_im
        map_re = maps_ref[rows, pl.ds(start, WINDOW)].astype(jnp.float32)
        map_im = maps_ref[rows, pl.ds(pl.multiple_of(start + pixels, LANES), WINDOW)].astype(
            jnp.float32
        )
        first = jnp.where(imaginary, -map_im, map_re) * factor
        second = jnp.where(imaginary, map_re, map_im) * factor
        term = first * sum_re + second * sum_im
        term = pltpu.roll(term, lax.rem(WINDOW - shift, WINDOW), 1)
        term_ref[rows, :] = term[:, :width]
    own_copy.wait()


def local_terms(seg_total, coil_total, image, maps, field, rows, cols, measured, time, count):
    pixels = field.shape[0]
    row_total, col_total = rows.shape[0], cols.shape[0]
    width = 2 * pixels // seg_total
    fourier = jnp.asarray(dft_tables(pixels), jnp.bfloat16)
    anywhere = pl.BlockSpec(memory_space=pl.ANY)
    vmem = pl.BlockSpec(memory_space=pltpu.VMEM)
    smem = pl.BlockSpec(memory_space=pltpu.SMEM)
    operands = (rows, fourier, cols, field, maps, image, measured)
    return pl.pallas_call(
        functools.partial(local_kernel, seg_total, coil_total, False),
        out_shape=(
            jax.ShapeDtypeStruct((pixels, width), jnp.float32),
            jax.ShapeDtypeStruct((row_total // seg_total, 2 * col_total), jnp.float32),
        ),
        in_specs=[smem, vmem] + [anywhere] * len(operands),
        out_specs=(vmem, anywhere),
        scratch_shapes=[pltpu.VMEM(x.shape, x.dtype) for x in operands]
        + [
            pltpu.VMEM((seg_total, pixels, 2 * pixels), jnp.bfloat16),
            pltpu.VMEM((seg_total, pixels, pixels), jnp.float32),
            pltpu.VMEM((2 * col_total, 2 * pixels), jnp.bfloat16),
            pltpu.VMEM((2 * pixels, 2 * col_total), jnp.bfloat16),
            pltpu.VMEM((row_total, 2 * col_total), jnp.float32),
            pltpu.VMEM((pixels, 2 * row_total), jnp.bfloat16),
            pltpu.VMEM((2 * row_total, 2 * WINDOW), jnp.bfloat16),
            pltpu.SemaphoreType.DMA((8,)),
        ],
        compiler_params=pltpu.CompilerParams(vmem_limit_bytes=56 * 1024 * 1024),
        name="local_terms",
    )(count, time, *operands)


def exchange_sum(blocks, axis):
    total = lax.axis_size(axis)
    me = lax.axis_index(axis)
    lane = me % 2
    group = me // 2
    groups = total // 2
    split = blocks.reshape(groups, 2, *blocks.shape[1:])
    away = lax.dynamic_index_in_dim(split, 1 - lane, 1, False)
    kept = lax.dynamic_index_in_dim(split, lane, 1, False)
    paired = kept + lax.ppermute(away, axis, [(i, i ^ 1) for i in range(total)])
    result = lax.dynamic_index_in_dim(paired, group, 0, False)
    for step in range(1, groups):
        piece = lax.dynamic_index_in_dim(paired, (group + step) % groups, 0, False)
        result = result + lax.ppermute(
            piece, axis, [(i, (i + 2 * step) % total) for i in range(total)]
        )
    return result


def shards(
    image_estimate,
    coil_maps,
    field_map,
    interp_rows,
    interp_cols,
    measured,
    sample_time,
    sample_count,
):
    seg_total = lax.axis_size("seg")
    coil_total = lax.axis_size("coil")
    pixels = field_map.shape[0]
    term, own = local_terms(
        seg_total,
        coil_total,
        image_estimate[0],
        coil_maps[0],
        field_map,
        interp_rows[0],
        interp_cols[0],
        measured[0, 0],
        sample_time,
        sample_count,
    )
    blocks = term.reshape(coil_total, pixels // coil_total, term.shape[1])
    gradient = exchange_sum(blocks, "coil")
    return gradient[None], own[None, None]


def solution(mesh):
    in_specs = (P(), P("coil", None, None), P(), P(), P(), P("coil", None, None, None), P(), P())
    out_specs = (P(None, "coil", "seg"), P("coil", None, "seg", None))
    return jax.shard_map(shards, mesh=mesh, in_specs=in_specs, out_specs=out_specs, check_vma=False)
```

```python
import functools
import math

import jax
import jax.numpy as jnp
import numpy as np
from jax import lax
from jax.experimental import pallas as pl
from jax.experimental.pallas import tpu as pltpu
from jax.sharding import PartitionSpec as P

SUBSTEPS = 4
LANES = 128
WINDOW = 256
CHUNK = 128
PIECE = 16
TALL = 48


def dft_tables(length):
    wrapped = np.outer(np.arange(length), np.arange(length)) % length
    angles = wrapped * (2.0 * math.pi / length)
    factor = 1.0 / math.sqrt(length)
    return np.concatenate([np.cos(angles) * factor, -np.sin(angles) * factor], 1)


def dot(a, b, contract=((1,), (0,))):
    return lax.dot_general(a, b, (contract, ((), ())), preferred_element_type=jnp.float32)


def sine_cosine(x):
    y = x * x
    sine = -1.0 / math.factorial(11)
    for power in (9, 7, 5, 3):
        sine = sine * y + (-1.0) ** (power // 2) / math.factorial(power)
    sine = x * (sine * y + 1.0)
    cosine = 1.0 / math.factorial(12)
    for power in (10, 8, 6, 4, 2):
        cosine = cosine * y + (-1.0) ** (power // 2) / math.factorial(power)
    return sine, cosine * y + 1.0


def pack(block):
    rows, width = block.shape
    if not packs(rows, width):
        return (block,)
    full = width - LANES // 2
    tail = jnp.concatenate([block[: rows // 2, full:], block[rows // 2 :, full:]], 1)
    return tuple(block[:, i : i + LANES] for i in range(0, full, LANES)) + (tail,)


def packs(rows, width):
    return width > LANES and width % LANES == LANES // 2 and rows % 16 == 0


def packed_shape(rows, width):
    return (rows * width // LANES, LANES) if packs(rows, width) else (rows, width)


def unpack(block, rows, width):
    if not packs(rows, width):
        return block
    full = width - LANES // 2
    count = full // LANES
    pieces = [block[i * rows : (i + 1) * rows] for i in range(count)]
    tail = block[count * rows :]
    pieces.append(jnp.concatenate([tail[:, : LANES // 2], tail[:, LANES // 2 :]], 0))
    return jnp.concatenate(pieces, 1)


def local_kernel(
    seg_total,
    coil_total,
    count_hbm,
    time_hbm,
    rows_hbm,
    fourier_hbm,
    cols_hbm,
    field_hbm,
    maps_hbm,
    image_hbm,
    measured_hbm,
    kept_ref,
    away_ref,
    own_ref,
    count_ref,
    time_ref,
    rows_ref,
    fourier_ref,
    cols_ref,
    field_ref,
    maps_ref,
    image_ref,
    measured_ref,
    wave_ref,
    phase_ref,
    left_ref,
    right_ref,
    inner_ref,
    misfit_ref,
    adjoint_ref,
    turned_ref,
    scaled_ref,
    back_ref,
    term_ref,
    sems,
):
    pixels = field_ref.shape[0]
    row_total = rows_ref.shape[0]
    col_total = cols_ref.shape[0]
    own_rows = row_total // seg_total
    width = 2 * pixels // seg_total
    pairs = seg_total // 2
    block_rows = pixels // coil_total
    groups = coil_total // 2
    segment = lax.axis_index("seg")
    member = lax.axis_index("coil")

    copies = [
        pltpu.make_async_copy(source, target, sems.at[i])
        for i, (source, target) in enumerate(
            (
                (rows_hbm, rows_ref),
                (fourier_hbm, fourier_ref),
                (cols_hbm, cols_ref),
                (time_hbm, time_ref),
                (field_hbm, field_ref),
                (maps_hbm, maps_ref),
                (image_hbm, image_ref),
                (measured_hbm, measured_ref),
                (count_hbm, count_ref),
            )
        )
    ]
    for copy in copies:
        copy.start()
    for copy in copies[:4]:
        copy.wait()

    grid_rows = rows_ref[...]
    grid_cols = cols_ref[...]
    fourier = fourier_ref[...]
    row_op = dot(grid_rows, fourier).astype(jnp.bfloat16)
    for part in range(2):
        span = slice(part * pixels, (part + 1) * pixels)
        adjoint_ref[:, part * row_total : (part + 1) * row_total] = dot(
            fourier[:, span], grid_rows, ((1,), (1,))
        ).astype(jnp.bfloat16)
    col_op = dot(grid_cols, fourier).astype(jnp.bfloat16)
    left_ref[:col_total, :pixels] = col_op[:, :pixels]
    left_ref[:col_total, pixels:] = -col_op[:, pixels:]
    left_ref[col_total:, :pixels] = col_op[:, pixels:]
    left_ref[col_total:, pixels:] = col_op[:, :pixels]
    col_re = dot(fourier[:, :pixels], grid_cols, ((1,), (1,))).astype(jnp.bfloat16)
    col_im = dot(fourier[:, pixels:], grid_cols, ((1,), (1,))).astype(jnp.bfloat16)
    right_ref[:pixels, :col_total] = col_re
    right_ref[:pixels, col_total:] = col_im
    right_ref[pixels:, :col_total] = -col_im
    right_ref[pixels:, col_total:] = col_re

    steps = jnp.broadcast_to(time_ref[...].astype(jnp.float32), (8, row_total))

    def weight(s):
        return jnp.maximum(0.0, 1.0 - jnp.abs(steps - float(s * SUBSTEPS)) / SUBSTEPS)

    along = []
    for pair in range(pairs):
        above, below = weight(pairs + pair), weight(pairs - 1 - pair)
        along += [above + below, above - below]
    adjoint = adjoint_ref[...]
    for i in range(seg_total):
        scale = jnp.concatenate([along[i][:1]] * 2, 1).astype(jnp.bfloat16)
        scaled_ref[i] = adjoint * scale

    for copy in copies[4:7]:
        copy.wait()
    right = right_ref[...]
    for chunk in range(pixels // CHUNK):
        for low in range(0, CHUNK, PIECE):
            rows = slice(chunk * CHUNK + low, chunk * CHUNK + low + PIECE)
            sine, cosine = sine_cosine(0.5 * field_ref[rows, :])
            image_re = image_ref[rows, :pixels].astype(jnp.float32)
            image_im = image_ref[rows, pixels:].astype(jnp.float32)
            map_re = maps_ref[rows, :pixels].astype(jnp.float32)
            map_im = maps_ref[rows, pixels:].astype(jnp.float32)
            base_re = image_re * map_re - image_im * map_im
            base_im = image_re * map_im + image_im * map_re
            twice_re = cosine * cosine - sine * sine
            twice_im = 2.0 * cosine * sine
            for pair in range(pairs):
                if pair:
                    cosine, sine = (
                        cosine * twice_re - sine * twice_im,
                        cosine * twice_im + sine * twice_re,
                    )
                phase_ref[2 * pair, rows, :] = cosine
                phase_ref[2 * pair + 1, rows, :] = sine
                even = slice(2 * pair * CHUNK + low, 2 * pair * CHUNK + low + PIECE)
                odd = slice(even.start + CHUNK, even.stop + CHUNK)
                wave_ref[chunk, even, :pixels] = (base_re * cosine).astype(jnp.bfloat16)
                wave_ref[chunk, even, pixels:] = (base_im * cosine).astype(jnp.bfloat16)
                wave_ref[chunk, odd, :pixels] = (-base_im * sine).astype(jnp.bfloat16)
                wave_ref[chunk, odd, pixels:] = (base_re * sine).astype(jnp.bfloat16)
        v = dot(wave_ref[chunk], right).astype(jnp.bfloat16)
        for i in range(seg_total):
            piece = v[i * CHUNK : (i + 1) * CHUNK]
            first = slice(chunk * CHUNK, (chunk + 1) * CHUNK)
            second = slice(pixels + first.start, pixels + first.stop)
            inner_ref[i, first, :] = piece
            inner_ref[i, second, :col_total] = -piece[:, col_total:]
            inner_ref[i, second, col_total:] = piece[:, :col_total]
    samples = None
    for i in range(seg_total):
        y = dot(row_op, inner_ref[i]) * jnp.transpose(along[i])[:, :1]
        samples = y if samples is None else samples + y

    copies[7].wait()
    copies[8].wait()
    row_ids = lax.broadcasted_iota(jnp.int32, (row_total, 2 * col_total), 0)
    misfit = samples - measured_ref[...].astype(jnp.float32)
    misfit = jnp.where(row_ids < count_ref[0], misfit, 0.0)
    misfit_ref[...] = misfit
    own_start = pl.multiple_of(segment * own_rows, own_rows)
    own_copy = pltpu.make_async_copy(misfit_ref.at[pl.ds(own_start, own_rows)], own_ref, sems.at[9])
    own_copy.start()

    column = lax.rem(segment * width, pixels)
    imaginary = segment * width >= pixels
    start = jnp.minimum(column // LANES * LANES, pixels - WINDOW)
    start = pl.multiple_of(start, LANES)
    after = pl.multiple_of(start + pixels, LANES)
    shift = lax.rem(WINDOW - (column - start), WINDOW)
    misfit = misfit.astype(jnp.bfloat16)
    turn_re = dot(misfit, left_ref[:, pl.ds(start, WINDOW)]).astype(jnp.bfloat16)
    turn_im = dot(misfit, left_ref[:, pl.ds(after, WINDOW)]).astype(jnp.bfloat16)
    turned_ref[:row_total, :WINDOW] = turn_re
    turned_ref[:row_total, WINDOW:] = turn_im
    turned_ref[row_total:, :WINDOW] = turn_im
    turned_ref[row_total:, WINDOW:] = -turn_re
    turned = turned_ref[...]
    factor = coil_total ** (-0.5)
    for i in range(seg_total):
        back_ref[i] = dot(scaled_ref[i], turned)
    for low in range(0, pixels, TALL):
        rows = slice(low, low + TALL)
        sum_re = None
        for pair in range(pairs):
            cosine = phase_ref[2 * pair, rows, pl.ds(start, WINDOW)]
            sine = phase_ref[2 * pair + 1, rows, pl.ds(start, WINDOW)]
            add_re = cosine * back_ref[2 * pair, rows, :WINDOW]
            add_re = add_re + sine * back_ref[2 * pair + 1, rows, WINDOW:]
            add_im = cosine * back_ref[2 * pair, rows, WINDOW:]
            add_im = add_im - sine * back_ref[2 * pair + 1, rows, :WINDOW]
            sum_re = add_re if sum_re is None else sum_re + add_re
            sum_im = add_im if pair == 0 else sum_im + add_im
        map_re = maps_ref[rows, pl.ds(start, WINDOW)].astype(jnp.float32)
        map_im = maps_ref[rows, pl.ds(after, WINDOW)].astype(jnp.float32)
        first = jnp.where(imaginary, -map_im, map_re) * factor
        second = jnp.where(imaginary, map_re, map_im) * factor
        term_ref[rows, :] = pltpu.roll(first * sum_re + second * sum_im, shift, 1)

    lane = lax.rem(member, 2)
    group = member // 2
    for g in range(groups):
        slot = lax.rem(g + groups - group, groups)
        upper = term_ref[2 * g * block_rows : (2 * g + 1) * block_rows, :width]
        lower = term_ref[(2 * g + 1) * block_rows : (2 * g + 2) * block_rows, :width]
        for ref, value in (
            (kept_ref, jnp.where(lane == 0, upper, lower)),
            (away_ref, jnp.where(lane == 0, lower, upper)),
        ):
            top = 0
            for piece in pack(value):
                ref[slot, top : top + piece.shape[0], :] = piece
                top += piece.shape[0]
    own_copy.wait()


def local_terms(seg_total, coil_total, image, maps, field, rows, cols, measured, time, count):
    pixels = field.shape[0]
    row_total, col_total = rows.shape[0], cols.shape[0]
    width = 2 * pixels // seg_total
    fourier = jnp.asarray(dft_tables(pixels), jnp.bfloat16)
    anywhere = pl.BlockSpec(memory_space=pl.ANY)
    vmem = pl.BlockSpec(memory_space=pltpu.VMEM)
    operands = (time, rows, fourier, cols, field, maps, image, measured)
    blocks = (coil_total // 2, *packed_shape(pixels // coil_total, width))
    return pl.pallas_call(
        functools.partial(local_kernel, seg_total, coil_total),
        out_shape=(
            pltpu.VMEM(blocks, jnp.float32),
            pltpu.VMEM(blocks, jnp.float32),
            jax.ShapeDtypeStruct((row_total // seg_total, 2 * col_total), jnp.float32),
        ),
        in_specs=[anywhere] * (1 + len(operands)),
        out_specs=(vmem, vmem, anywhere),
        scratch_shapes=[pltpu.SMEM(count.shape, count.dtype)]
        + [pltpu.VMEM(x.shape, x.dtype) for x in operands]
        + [
            pltpu.VMEM((pixels // CHUNK, seg_total * CHUNK, 2 * pixels), jnp.bfloat16),
            pltpu.VMEM((seg_total, pixels, pixels), jnp.float32),
            pltpu.VMEM((2 * col_total, 2 * pixels), jnp.bfloat16),
            pltpu.VMEM((2 * pixels, 2 * col_total), jnp.bfloat16),
            pltpu.VMEM((seg_total, 2 * pixels, 2 * col_total), jnp.bfloat16),
            pltpu.VMEM((row_total, 2 * col_total), jnp.float32),
            pltpu.VMEM((pixels, 2 * row_total), jnp.bfloat16),
            pltpu.VMEM((2 * row_total, 2 * WINDOW), jnp.bfloat16),
            pltpu.VMEM((seg_total, pixels, 2 * row_total), jnp.bfloat16),
            pltpu.VMEM((seg_total, pixels, 2 * WINDOW), jnp.float32),
            pltpu.VMEM((pixels, WINDOW), jnp.float32),
            pltpu.SemaphoreType.DMA((10,)),
        ],
        compiler_params=pltpu.CompilerParams(vmem_limit_bytes=56 * 1024 * 1024),
        name="local_terms",
    )(count, *operands)


def exchange_sum(kept, away, axis):
    total = lax.axis_size(axis)
    paired = kept + lax.ppermute(away, axis, [(i, i ^ 1) for i in range(total)])
    result = paired[0]
    for step in range(1, total // 2):
        result = result + lax.ppermute(
            paired[step], axis, [(i, (i + 2 * step) % total) for i in range(total)]
        )
    return result


def shards(
    image_estimate,
    coil_maps,
    field_map,
    interp_rows,
    interp_cols,
    measured,
    sample_time,
    sample_count,
):
    seg_total = lax.axis_size("seg")
    coil_total = lax.axis_size("coil")
    pixels = field_map.shape[0]
    kept, away, own = local_terms(
        seg_total,
        coil_total,
        image_estimate[0],
        coil_maps[0],
        field_map,
        interp_rows[0],
        interp_cols[0],
        measured[0, 0],
        sample_time,
        sample_count,
    )
    total = exchange_sum(kept, away, "coil")
    gradient = unpack(total, pixels // coil_total, 2 * pixels // seg_total)
    return gradient[None], own[None, None]


def solution(mesh):
    in_specs = (P(), P("coil", None, None), P(), P(), P(), P("coil", None, None, None), P(), P())
    out_specs = (P(None, "coil", "seg"), P("coil", None, "seg", None))
    return jax.shard_map(shards, mesh=mesh, in_specs=in_specs, out_specs=out_specs, check_vma=False)
```

```python
import functools
import math

import jax
import jax.numpy as jnp
import numpy as np
from jax import lax
from jax.experimental import pallas as pl
from jax.experimental.pallas import tpu as pltpu
from jax.sharding import PartitionSpec as P

SUBSTEPS = 4
LANES = 128
WINDOW = 256
CHUNK = 192
HALF = 192
PIECE = 16


def dft_tables(length):
    wrapped = np.outer(np.arange(length), np.arange(length)) % length
    angles = wrapped * (2.0 * math.pi / length)
    factor = 1.0 / math.sqrt(length)
    return np.concatenate([np.cos(angles) * factor, -np.sin(angles) * factor], 1)


def dot(a, b, contract=((1,), (0,))):
    return lax.dot_general(a, b, (contract, ((), ())), preferred_element_type=jnp.float32)


SINE = (
    0.49999999863922073,
    -0.020833325771248395,
    0.00026040993453922765,
    -1.5479976876565651e-06,
    5.113416832465264e-09,
)
COSINE = (
    0.999999999872559,
    -0.12499999898030063,
    0.002604165343651872,
    -2.170076051907257e-05,
    9.674607230271745e-08,
    -2.5566742521071554e-10,
)


def polynomial(terms, z):
    total = terms[-1] * z + terms[-2]
    for term in terms[-3::-1]:
        total = total * z + term
    return total


def half_angle(field):
    z = field * field
    return field * polynomial(SINE, z), polynomial(COSINE, z)


def pack(block):
    rows, width = block.shape
    if not packs(rows, width):
        return (block,)
    full = width - LANES // 2
    tail = jnp.concatenate([block[: rows // 2, full:], block[rows // 2 :, full:]], 1)
    return tuple(block[:, i : i + LANES] for i in range(0, full, LANES)) + (tail,)


def packs(rows, width):
    return width > LANES and width % LANES == LANES // 2 and rows % 16 == 0


def packed_shape(rows, width):
    return (rows * width // LANES, LANES) if packs(rows, width) else (rows, width)


def unpack(block, rows, width):
    if not packs(rows, width):
        return block
    full = width - LANES // 2
    count = full // LANES
    pieces = [block[i * rows : (i + 1) * rows] for i in range(count)]
    tail = block[count * rows :]
    pieces.append(jnp.concatenate([tail[:, : LANES // 2], tail[:, LANES // 2 :]], 0))
    return jnp.concatenate(pieces, 1)


def local_kernel(
    seg_total,
    coil_total,
    count_hbm,
    time_hbm,
    rows_hbm,
    fourier_hbm,
    cols_hbm,
    field_hbm,
    maps_hbm,
    image_hbm,
    measured_hbm,
    kept_ref,
    away_ref,
    own_ref,
    count_ref,
    time_ref,
    rows_ref,
    fourier_ref,
    cols_ref,
    field_ref,
    maps_ref,
    image_ref,
    measured_ref,
    wave_ref,
    phase_ref,
    left_ref,
    right_ref,
    inner_ref,
    misfit_ref,
    row_ref,
    turned_ref,
    scaled_ref,
    back_ref,
    term_ref,
    sems,
):
    pixels = field_ref.shape[0]
    row_total = rows_ref.shape[0]
    col_total = cols_ref.shape[0]
    own_rows = row_total // seg_total
    width = 2 * pixels // seg_total
    pairs = seg_total // 2
    block_rows = pixels // coil_total
    groups = coil_total // 2
    segment = lax.axis_index("seg")
    member = lax.axis_index("coil")

    copies = [
        pltpu.make_async_copy(source, target, sems.at[i])
        for i, (source, target) in enumerate(
            (
                (rows_hbm, rows_ref),
                (fourier_hbm, fourier_ref),
                (cols_hbm, cols_ref),
                (time_hbm, time_ref),
                (field_hbm, field_ref),
                (maps_hbm, maps_ref),
                (image_hbm, image_ref),
                (measured_hbm, measured_ref),
                (count_hbm, count_ref),
            )
        )
    ]
    for copy in copies:
        copy.start()
    for copy in copies[:5]:
        copy.wait()

    fourier = fourier_ref[...]
    row_op = dot(rows_ref[...], fourier).astype(jnp.bfloat16)
    row_ref[...] = row_op
    col_op = dot(cols_ref[...], fourier).astype(jnp.bfloat16)
    left_ref[:col_total, :pixels] = col_op[:, :pixels]
    left_ref[:col_total, pixels:] = -col_op[:, pixels:]
    left_ref[col_total:, :pixels] = col_op[:, pixels:]
    left_ref[col_total:, pixels:] = col_op[:, :pixels]
    col_re = jnp.transpose(col_op[:, :pixels])
    col_im = jnp.transpose(col_op[:, pixels:])
    right_ref[:pixels, :col_total] = col_re
    right_ref[:pixels, col_total:] = col_im
    right_ref[pixels:, :col_total] = -col_im
    right_ref[pixels:, col_total:] = col_re

    for low in range(0, pixels, PIECE):
        rows = slice(low, low + PIECE)
        sine, cosine = half_angle(field_ref[rows, :])
        twice = 4.0 * (cosine * cosine) - 2.0
        previous = (cosine, -sine)
        for pair in range(pairs):
            if pair == 1:
                previous, cosine, sine = (
                    (cosine, sine),
                    twice * cosine - cosine,
                    twice * sine + sine,
                )
            elif pair:
                previous, cosine, sine = (
                    (cosine, sine),
                    twice * cosine - previous[0],
                    twice * sine - previous[1],
                )
            phase_ref[2 * pair, rows, :] = cosine
            phase_ref[2 * pair + 1, rows, :] = sine

    steps = jnp.broadcast_to(time_ref[...].astype(jnp.float32), (8, row_total))

    def weight(s):
        return jnp.maximum(0.0, 1.0 - jnp.abs(steps - float(s * SUBSTEPS)) / SUBSTEPS)

    along = []
    for pair in range(pairs):
        above, below = weight(pairs + pair), weight(pairs - 1 - pair)
        along += [above + below, above - below]
    for part in range(2):
        adjoint = jnp.transpose(row_op[:, part * pixels : (part + 1) * pixels])
        columns = slice(part * row_total, (part + 1) * row_total)
        for i in range(seg_total):
            scaled = adjoint * along[i][:1].astype(jnp.bfloat16)
            for half in range(pixels // HALF):
                scaled_ref[half, i * HALF : (i + 1) * HALF, columns] = scaled[
                    half * HALF : (half + 1) * HALF
                ]

    for copy in copies[5:7]:
        copy.wait()
    right = right_ref[...]
    for chunk in range(pixels // CHUNK):
        for low in range(0, CHUNK, PIECE):
            rows = slice(chunk * CHUNK + low, chunk * CHUNK + low + PIECE)
            image_re, image_im = image_ref[rows, :pixels], image_ref[rows, pixels:]
            map_re, map_im = maps_ref[rows, :pixels], maps_ref[rows, pixels:]
            base_re = image_re * map_re - image_im * map_im
            base_im = image_re * map_im + image_im * map_re
            for pair in range(pairs):
                cosine = phase_ref[2 * pair, rows, :].astype(jnp.bfloat16)
                sine = phase_ref[2 * pair + 1, rows, :].astype(jnp.bfloat16)
                even = slice(2 * pair * CHUNK + low, 2 * pair * CHUNK + low + PIECE)
                odd = slice(even.start + CHUNK, even.stop + CHUNK)
                wave_ref[chunk, even, :pixels] = base_re * cosine
                wave_ref[chunk, even, pixels:] = base_im * cosine
                wave_ref[chunk, odd, :pixels] = -base_im * sine
                wave_ref[chunk, odd, pixels:] = base_re * sine
        v = dot(wave_ref[chunk], right).astype(jnp.bfloat16)
        for i in range(seg_total):
            piece = v[i * CHUNK : (i + 1) * CHUNK]
            first = slice(chunk * CHUNK, (chunk + 1) * CHUNK)
            second = slice(pixels + first.start, pixels + first.stop)
            inner_ref[i, first, :] = piece
            inner_ref[i, second, :col_total] = -piece[:, col_total:]
            inner_ref[i, second, col_total:] = piece[:, :col_total]
    samples = None
    for i in range(seg_total):
        y = dot(row_ref[...], inner_ref[i]) * jnp.transpose(along[i])[:, :1]
        samples = y if samples is None else samples + y

    copies[7].wait()
    copies[8].wait()
    row_ids = lax.broadcasted_iota(jnp.int32, (row_total, 2 * col_total), 0)
    misfit = samples - measured_ref[...].astype(jnp.float32)
    misfit = jnp.where(row_ids < count_ref[...], misfit, 0.0)
    misfit_ref[...] = misfit
    own_start = pl.multiple_of(segment * own_rows, own_rows)
    own_copy = pltpu.make_async_copy(misfit_ref.at[pl.ds(own_start, own_rows)], own_ref, sems.at[9])
    own_copy.start()

    column = lax.rem(segment * width, pixels)
    imaginary = segment * width >= pixels
    start = jnp.minimum(column // LANES * LANES, pixels - WINDOW)
    start = pl.multiple_of(start, LANES)
    after = pl.multiple_of(start + pixels, LANES)
    shift = lax.rem(WINDOW - (column - start), WINDOW)
    misfit = misfit.astype(jnp.bfloat16)
    turn_re = dot(misfit, left_ref[:, pl.ds(start, WINDOW)]).astype(jnp.bfloat16)
    turn_im = dot(misfit, left_ref[:, pl.ds(after, WINDOW)]).astype(jnp.bfloat16)
    turned_ref[:row_total, :WINDOW] = turn_re
    turned_ref[:row_total, WINDOW:] = turn_im
    turned_ref[row_total:, :WINDOW] = turn_im
    turned_ref[row_total:, WINDOW:] = -turn_re
    turned = turned_ref[...]
    factor = coil_total ** (-0.5)
    for half in range(pixels // HALF):
        back_ref[half] = dot(scaled_ref[half], turned)
        for low in range(0, HALF, PIECE):
            rows = slice(half * HALF + low, half * HALF + low + PIECE)
            sum_re = None
            for pair in range(pairs):
                cosine = phase_ref[2 * pair, rows, pl.ds(start, WINDOW)]
                sine = phase_ref[2 * pair + 1, rows, pl.ds(start, WINDOW)]
                even = slice(2 * pair * HALF + low, 2 * pair * HALF + low + PIECE)
                odd = slice(even.start + HALF, even.stop + HALF)
                add_re = cosine * back_ref[half, even, :WINDOW]
                add_re = add_re + sine * back_ref[half, odd, WINDOW:]
                add_im = cosine * back_ref[half, even, WINDOW:]
                add_im = add_im - sine * back_ref[half, odd, :WINDOW]
                sum_re = add_re if sum_re is None else sum_re + add_re
                sum_im = add_im if pair == 0 else sum_im + add_im
            map_re = maps_ref[rows, pl.ds(start, WINDOW)].astype(jnp.float32)
            map_im = maps_ref[rows, pl.ds(after, WINDOW)].astype(jnp.float32)
            first = jnp.where(imaginary, -map_im, map_re) * factor
            second = jnp.where(imaginary, map_re, map_im) * factor
            term_ref[rows, :] = pltpu.roll(first * sum_re + second * sum_im, shift, 1)

    lane = lax.rem(member, 2)
    group = member // 2
    for g in range(groups):
        slot = lax.rem(g + groups - group, groups)
        upper = term_ref[2 * g * block_rows : (2 * g + 1) * block_rows, :width]
        lower = term_ref[(2 * g + 1) * block_rows : (2 * g + 2) * block_rows, :width]
        for ref, value in (
            (kept_ref, jnp.where(lane == 0, upper, lower)),
            (away_ref, jnp.where(lane == 0, lower, upper)),
        ):
            top = 0
            for piece in pack(value):
                ref[slot, top : top + piece.shape[0], :] = piece
                top += piece.shape[0]
    own_copy.wait()


def local_terms(seg_total, coil_total, image, maps, field, rows, cols, measured, time, count):
    pixels = field.shape[0]
    row_total, col_total = rows.shape[0], cols.shape[0]
    width = 2 * pixels // seg_total
    fourier = jnp.asarray(dft_tables(pixels), jnp.bfloat16)
    anywhere = pl.BlockSpec(memory_space=pl.ANY)
    vmem = pl.BlockSpec(memory_space=pltpu.VMEM)
    operands = (time, rows, fourier, cols, field, maps, image, measured)
    blocks = (coil_total // 2, *packed_shape(pixels // coil_total, width))
    return pl.pallas_call(
        functools.partial(local_kernel, seg_total, coil_total),
        out_shape=(
            pltpu.VMEM(blocks, jnp.float32),
            pltpu.VMEM(blocks, jnp.float32),
            jax.ShapeDtypeStruct((row_total // seg_total, 2 * col_total), jnp.float32),
        ),
        in_specs=[anywhere] * (1 + len(operands)),
        out_specs=(vmem, vmem, anywhere),
        scratch_shapes=[pltpu.VMEM(x.shape, x.dtype) for x in (count, *operands)]
        + [
            pltpu.VMEM((pixels // CHUNK, seg_total * CHUNK, 2 * pixels), jnp.bfloat16),
            pltpu.VMEM((seg_total, pixels, pixels), jnp.float32),
            pltpu.VMEM((2 * col_total, 2 * pixels), jnp.bfloat16),
            pltpu.VMEM((2 * pixels, 2 * col_total), jnp.bfloat16),
            pltpu.VMEM((seg_total, 2 * pixels, 2 * col_total), jnp.bfloat16),
            pltpu.VMEM((row_total, 2 * col_total), jnp.float32),
            pltpu.VMEM((row_total, 2 * pixels), jnp.bfloat16),
            pltpu.VMEM((2 * row_total, 2 * WINDOW), jnp.bfloat16),
            pltpu.VMEM((pixels // HALF, seg_total * HALF, 2 * row_total), jnp.bfloat16),
            pltpu.VMEM((pixels // HALF, seg_total * HALF, 2 * WINDOW), jnp.float32),
            pltpu.VMEM((pixels, WINDOW), jnp.float32),
            pltpu.SemaphoreType.DMA((10,)),
        ],
        compiler_params=pltpu.CompilerParams(vmem_limit_bytes=56 * 1024 * 1024),
        name="local_terms",
    )(count, *operands)


def exchange_sum(kept, away, axis):
    total = lax.axis_size(axis)
    paired = kept + lax.ppermute(away, axis, [(i, i ^ 1) for i in range(total)])
    result = paired[0]
    for step in range(1, total // 2):
        result = result + lax.ppermute(
            paired[step], axis, [(i, (i + 2 * step) % total) for i in range(total)]
        )
    return result


def shards(
    image_estimate,
    coil_maps,
    field_map,
    interp_rows,
    interp_cols,
    measured,
    sample_time,
    sample_count,
):
    seg_total = lax.axis_size("seg")
    coil_total = lax.axis_size("coil")
    pixels = field_map.shape[0]
    kept, away, own = local_terms(
        seg_total,
        coil_total,
        image_estimate[0],
        coil_maps[0],
        field_map,
        interp_rows[0],
        interp_cols[0],
        measured[0, 0],
        sample_time,
        sample_count.reshape(1, 1),
    )
    total = exchange_sum(kept, away, "coil")
    gradient = unpack(total, pixels // coil_total, 2 * pixels // seg_total)
    return gradient[None], own[None, None]


def solution(mesh):
    in_specs = (P(), P("coil", None, None), P(), P(), P(), P("coil", None, None, None), P(), P())
    out_specs = (P(None, "coil", "seg"), P("coil", None, "seg", None))
    return jax.shard_map(shards, mesh=mesh, in_specs=in_specs, out_specs=out_specs, check_vma=False)
```

```python
import functools
import math

import jax
import jax.numpy as jnp
import numpy as np
from jax import lax
from jax.experimental import pallas as pl
from jax.experimental.pallas import tpu as pltpu
from jax.sharding import PartitionSpec as P

SUBSTEPS = 4
LANES = 128
WINDOW = 256
CHUNK = 192
HALF = 192
PIECE = 16


def dft_tables(length):
    wrapped = np.outer(np.arange(length), np.arange(length)) % length
    angles = wrapped * (2.0 * math.pi / length)
    factor = 1.0 / math.sqrt(length)
    return np.concatenate([np.cos(angles) * factor, -np.sin(angles) * factor], 1)


def dot(a, b, contract=((1,), (0,))):
    return lax.dot_general(a, b, (contract, ((), ())), preferred_element_type=jnp.float32)


SINE = (
    0.49999999863922073,
    -0.020833325771248395,
    0.00026040993453922765,
    -1.5479976876565651e-06,
    5.113416832465264e-09,
)
COSINE = (
    0.999999999872559,
    -0.12499999898030063,
    0.002604165343651872,
    -2.170076051907257e-05,
    9.674607230271745e-08,
    -2.5566742521071554e-10,
)


def polynomial(terms, z):
    total = terms[-1] * z + terms[-2]
    for term in terms[-3::-1]:
        total = total * z + term
    return total


def half_angle(field):
    z = field * field
    return field * polynomial(SINE, z), polynomial(COSINE, z)


def pack(block):
    rows, width = block.shape
    if not packs(rows, width):
        return (block,)
    full = width - LANES // 2
    tail = jnp.concatenate([block[: rows // 2, full:], block[rows // 2 :, full:]], 1)
    return tuple(block[:, i : i + LANES] for i in range(0, full, LANES)) + (tail,)


def packs(rows, width):
    return width > LANES and width % LANES == LANES // 2 and rows % 16 == 0


def packed_shape(rows, width):
    return (rows * width // LANES, LANES) if packs(rows, width) else (rows, width)


def unpack(block, rows, width):
    if not packs(rows, width):
        return block
    full = width - LANES // 2
    count = full // LANES
    pieces = [block[i * rows : (i + 1) * rows] for i in range(count)]
    tail = block[count * rows :]
    pieces.append(jnp.concatenate([tail[:, : LANES // 2], tail[:, LANES // 2 :]], 0))
    return jnp.concatenate(pieces, 1)


def local_kernel(
    seg_total,
    coil_total,
    count_hbm,
    time_hbm,
    rows_hbm,
    fourier_hbm,
    cols_hbm,
    field_hbm,
    maps_hbm,
    image_hbm,
    measured_hbm,
    kept_ref,
    away_ref,
    own_ref,
    count_ref,
    time_ref,
    rows_ref,
    fourier_ref,
    cols_ref,
    field_ref,
    maps_ref,
    image_ref,
    measured_ref,
    wave_ref,
    phase_ref,
    left_ref,
    right_ref,
    inner_ref,
    misfit_ref,
    row_ref,
    turned_ref,
    scaled_ref,
    back_ref,
    term_ref,
    sems,
):
    pixels = field_ref.shape[0]
    row_total = rows_ref.shape[0]
    col_total = cols_ref.shape[0]
    own_rows = row_total // seg_total
    width = 2 * pixels // seg_total
    pairs = seg_total // 2
    block_rows = pixels // coil_total
    groups = coil_total // 2
    segment = lax.axis_index("seg")
    member = lax.axis_index("coil")

    copies = [
        pltpu.make_async_copy(source, target, sems.at[i])
        for i, (source, target) in enumerate(
            (
                (rows_hbm, rows_ref),
                (fourier_hbm, fourier_ref),
                (cols_hbm, cols_ref),
                (time_hbm, time_ref),
                (field_hbm, field_ref),
                (maps_hbm, maps_ref),
                (image_hbm, image_ref),
                (measured_hbm, measured_ref),
                (count_hbm, count_ref),
            )
        )
    ]
    for copy in copies:
        copy.start()
    for copy in copies[:5]:
        copy.wait()

    fourier = fourier_ref[...]
    row_op = dot(rows_ref[...], fourier).astype(jnp.bfloat16)
    row_ref[...] = row_op
    col_op = dot(cols_ref[...], fourier).astype(jnp.bfloat16)
    left_ref[:col_total, :pixels] = col_op[:, :pixels]
    left_ref[:col_total, pixels:] = -col_op[:, pixels:]
    left_ref[col_total:, :pixels] = col_op[:, pixels:]
    left_ref[col_total:, pixels:] = col_op[:, :pixels]
    col_re = jnp.transpose(col_op[:, :pixels])
    col_im = jnp.transpose(col_op[:, pixels:])
    right_ref[:pixels, :col_total] = col_re
    right_ref[:pixels, col_total:] = col_im
    right_ref[pixels:, :col_total] = -col_im
    right_ref[pixels:, col_total:] = col_re

    for low in range(0, pixels, PIECE):
        rows = slice(low, low + PIECE)
        sine, cosine = half_angle(field_ref[rows, :])
        twice = 4.0 * (cosine * cosine) - 2.0
        previous = (cosine, -sine)
        for pair in range(pairs):
            if pair == 1:
                previous, cosine, sine = (
                    (cosine, sine),
                    twice * cosine - cosine,
                    twice * sine + sine,
                )
            elif pair:
                previous, cosine, sine = (
                    (cosine, sine),
                    twice * cosine - previous[0],
                    twice * sine - previous[1],
                )
            phase_ref[2 * pair, rows, :] = cosine
            phase_ref[2 * pair + 1, rows, :] = sine

    steps = jnp.broadcast_to(time_ref[...].astype(jnp.float32), (8, row_total))

    def weight(s):
        return jnp.maximum(0.0, 1.0 - jnp.abs(steps - float(s * SUBSTEPS)) / SUBSTEPS)

    along = []
    for pair in range(pairs):
        above, below = weight(pairs + pair), weight(pairs - 1 - pair)
        along += [above + below, above - below]
    for part in range(2):
        adjoint = jnp.transpose(row_op[:, part * pixels : (part + 1) * pixels])
        columns = slice(part * row_total, (part + 1) * row_total)
        for i in range(seg_total):
            scaled = adjoint * along[i][:1].astype(jnp.bfloat16)
            for half in range(pixels // HALF):
                scaled_ref[half, i * HALF : (i + 1) * HALF, columns] = scaled[
                    half * HALF : (half + 1) * HALF
                ]

    for copy in copies[5:7]:
        copy.wait()
    right = right_ref[...]
    for chunk in range(pixels // CHUNK):
        for low in range(0, CHUNK, PIECE):
            rows = slice(chunk * CHUNK + low, chunk * CHUNK + low + PIECE)
            image_re, image_im = image_ref[rows, :pixels], image_ref[rows, pixels:]
            map_re, map_im = maps_ref[rows, :pixels], maps_ref[rows, pixels:]
            base_re = image_re * map_re - image_im * map_im
            base_im = image_re * map_im + image_im * map_re
            for pair in range(pairs):
                cosine = phase_ref[2 * pair, rows, :].astype(jnp.bfloat16)
                sine = phase_ref[2 * pair + 1, rows, :].astype(jnp.bfloat16)
                even = slice(2 * pair * CHUNK + low, 2 * pair * CHUNK + low + PIECE)
                odd = slice(even.start + CHUNK, even.stop + CHUNK)
                wave_ref[chunk, even, :pixels] = base_re * cosine
                wave_ref[chunk, even, pixels:] = base_im * cosine
                wave_ref[chunk, odd, :pixels] = -base_im * sine
                wave_ref[chunk, odd, pixels:] = base_re * sine
        v = dot(wave_ref[chunk], right).astype(jnp.bfloat16)
        for i in range(seg_total):
            piece = v[i * CHUNK : (i + 1) * CHUNK]
            first = slice(chunk * CHUNK, (chunk + 1) * CHUNK)
            second = slice(pixels + first.start, pixels + first.stop)
            inner_ref[i, first, :] = piece
            inner_ref[i, second, :col_total] = -piece[:, col_total:]
            inner_ref[i, second, col_total:] = piece[:, :col_total]
    samples = None
    for i in range(seg_total):
        y = dot(row_ref[...], inner_ref[i]) * jnp.transpose(along[i])[:, :1]
        samples = y if samples is None else samples + y

    copies[7].wait()
    copies[8].wait()
    row_ids = lax.broadcasted_iota(jnp.int32, (row_total, 2 * col_total), 0)
    misfit = samples - measured_ref[...].astype(jnp.float32)
    misfit = jnp.where(row_ids < count_ref[...], misfit, 0.0)
    misfit_ref[...] = misfit
    own_start = pl.multiple_of(segment * own_rows, own_rows)
    own_copy = pltpu.make_async_copy(misfit_ref.at[pl.ds(own_start, own_rows)], own_ref, sems.at[9])
    own_copy.start()

    column = lax.rem(segment * width, pixels)
    imaginary = segment * width >= pixels
    start = jnp.minimum(column // LANES * LANES, pixels - WINDOW)
    start = pl.multiple_of(start, LANES)
    after = pl.multiple_of(start + pixels, LANES)
    shift = lax.rem(WINDOW - (column - start), WINDOW)
    misfit = misfit.astype(jnp.bfloat16)
    turn_re = dot(misfit, left_ref[:, pl.ds(start, WINDOW)]).astype(jnp.bfloat16)
    turn_im = dot(misfit, left_ref[:, pl.ds(after, WINDOW)]).astype(jnp.bfloat16)
    turned_ref[:row_total, :WINDOW] = turn_re
    turned_ref[:row_total, WINDOW:] = turn_im
    turned_ref[row_total:, :WINDOW] = turn_im
    turned_ref[row_total:, WINDOW:] = -turn_re
    turned = turned_ref[...]
    factor = coil_total ** (-0.5)
    for half in range(pixels // HALF):
        back_ref[half] = dot(scaled_ref[half], turned)
        for low in range(0, HALF, PIECE):
            rows = slice(half * HALF + low, half * HALF + low + PIECE)
            sum_re = None
            for pair in range(pairs):
                cosine = phase_ref[2 * pair, rows, pl.ds(start, WINDOW)]
                sine = phase_ref[2 * pair + 1, rows, pl.ds(start, WINDOW)]
                even = slice(2 * pair * HALF + low, 2 * pair * HALF + low + PIECE)
                odd = slice(even.start + HALF, even.stop + HALF)
                add_re = cosine * back_ref[half, even, :WINDOW]
                add_re = add_re + sine * back_ref[half, odd, WINDOW:]
                add_im = cosine * back_ref[half, even, WINDOW:]
                add_im = add_im - sine * back_ref[half, odd, :WINDOW]
                sum_re = add_re if sum_re is None else sum_re + add_re
                sum_im = add_im if pair == 0 else sum_im + add_im
            map_re = maps_ref[rows, pl.ds(start, WINDOW)].astype(jnp.float32)
            map_im = maps_ref[rows, pl.ds(after, WINDOW)].astype(jnp.float32)
            first = jnp.where(imaginary, -map_im, map_re) * factor
            second = jnp.where(imaginary, map_re, map_im) * factor
            term_ref[rows, :] = pltpu.roll(first * sum_re + second * sum_im, shift, 1)

    lane = lax.rem(member, 2)
    group = member // 2
    for g in range(groups):
        slot = slot_of(g, group, groups)
        upper = term_ref[2 * g * block_rows : (2 * g + 1) * block_rows, :width]
        lower = term_ref[(2 * g + 1) * block_rows : (2 * g + 2) * block_rows, :width]
        for ref, value in (
            (kept_ref, jnp.where(lane == 0, upper, lower)),
            (away_ref, jnp.where(lane == 0, lower, upper)),
        ):
            top = 0
            for piece in pack(value):
                ref[slot, top : top + piece.shape[0], :] = piece
                top += piece.shape[0]
    own_copy.wait()


def local_terms(seg_total, coil_total, image, maps, field, rows, cols, measured, time, count):
    pixels = field.shape[0]
    row_total, col_total = rows.shape[0], cols.shape[0]
    width = 2 * pixels // seg_total
    fourier = jnp.asarray(dft_tables(pixels), jnp.bfloat16)
    anywhere = pl.BlockSpec(memory_space=pl.ANY)
    vmem = pl.BlockSpec(memory_space=pltpu.VMEM)
    operands = (time, rows, fourier, cols, field, maps, image, measured)
    blocks = (coil_total // 2, *packed_shape(pixels // coil_total, width))
    return pl.pallas_call(
        functools.partial(local_kernel, seg_total, coil_total),
        out_shape=(
            pltpu.VMEM(blocks, jnp.float32),
            pltpu.VMEM(blocks, jnp.float32),
            jax.ShapeDtypeStruct((row_total // seg_total, 2 * col_total), jnp.float32),
        ),
        in_specs=[anywhere] * (1 + len(operands)),
        out_specs=(vmem, vmem, anywhere),
        scratch_shapes=[pltpu.VMEM(x.shape, x.dtype) for x in (count, *operands)]
        + [
            pltpu.VMEM((pixels // CHUNK, seg_total * CHUNK, 2 * pixels), jnp.bfloat16),
            pltpu.VMEM((seg_total, pixels, pixels), jnp.float32),
            pltpu.VMEM((2 * col_total, 2 * pixels), jnp.bfloat16),
            pltpu.VMEM((2 * pixels, 2 * col_total), jnp.bfloat16),
            pltpu.VMEM((seg_total, 2 * pixels, 2 * col_total), jnp.bfloat16),
            pltpu.VMEM((row_total, 2 * col_total), jnp.float32),
            pltpu.VMEM((row_total, 2 * pixels), jnp.bfloat16),
            pltpu.VMEM((2 * row_total, 2 * WINDOW), jnp.bfloat16),
            pltpu.VMEM((pixels // HALF, seg_total * HALF, 2 * row_total), jnp.bfloat16),
            pltpu.VMEM((pixels // HALF, seg_total * HALF, 2 * WINDOW), jnp.float32),
            pltpu.VMEM((pixels, WINDOW), jnp.float32),
            pltpu.SemaphoreType.DMA((10,)),
        ],
        compiler_params=pltpu.CompilerParams(vmem_limit_bytes=56 * 1024 * 1024),
        name="local_terms",
    )(count, *operands)


def routes(groups):
    if groups == 4:
        return [(2, 3, 1, 0), (3, 2, 0, 1), (1, 0, 3, 2)]
    return [tuple((z + step) % groups for z in range(groups)) for step in range(1, groups)]


def slot_of(target, group, groups):
    if groups != 4:
        return lax.rem(target + groups - group, groups)
    slot = jnp.int32(0)
    for k, route in enumerate(routes(groups)):
        slot = jnp.where(group == route.index(target), k + 1, slot)
    return slot


def exchange_sum(kept, away, axis):
    total = lax.axis_size(axis)
    paired = kept + lax.ppermute(away, axis, [(i, i ^ 1) for i in range(total)])
    result = paired[0]
    for k, route in enumerate(routes(total // 2)):
        pairs = [(i, 2 * route[i // 2] + i % 2) for i in range(total)]
        got = lax.ppermute(paired[k + 1], axis, pairs)
        result = result + got
    return result


def shards(
    image_estimate,
    coil_maps,
    field_map,
    interp_rows,
    interp_cols,
    measured,
    sample_time,
    sample_count,
):
    seg_total = lax.axis_size("seg")
    coil_total = lax.axis_size("coil")
    pixels = field_map.shape[0]
    kept, away, own = local_terms(
        seg_total,
        coil_total,
        image_estimate[0],
        coil_maps[0],
        field_map,
        interp_rows[0],
        interp_cols[0],
        measured[0, 0],
        sample_time,
        sample_count.reshape(1, 1),
    )
    total = exchange_sum(kept, away, "coil")
    gradient = unpack(total, pixels // coil_total, 2 * pixels // seg_total)
    return gradient[None], own[None, None]


def solution(mesh):
    in_specs = (P(), P("coil", None, None), P(), P(), P(), P("coil", None, None, None), P(), P())
    out_specs = (P(None, "coil", "seg"), P("coil", None, "seg", None))
    return jax.shard_map(
        shards, mesh=mesh, in_specs=in_specs, out_specs=out_specs, check_vma=False
    )
```

```python
import functools
import math

import jax
import jax.numpy as jnp
import numpy as np
from jax import lax
from jax.experimental import pallas as pl
from jax.experimental.pallas import tpu as pltpu
from jax.sharding import PartitionSpec as P

SUBSTEPS = 4
LANES = 128
WINDOW = 256
CHUNK = 192
EARLY = 256
CUTS = (192, 384)
PIECE = 16


def dft_tables(length):
    wrapped = np.outer(np.arange(length), np.arange(length)) % length
    angles = wrapped * (2.0 * math.pi / length)
    factor = 1.0 / math.sqrt(length)
    return np.concatenate([np.cos(angles) * factor, -np.sin(angles) * factor], 1)


def dot(a, b, contract=((1,), (0,))):
    return lax.dot_general(a, b, (contract, ((), ())), preferred_element_type=jnp.float32)


SINE = (
    0.49999999863922073,
    -0.020833325771248395,
    0.00026040993453922765,
    -1.5479976876565651e-06,
    5.113416832465264e-09,
)
COSINE = (
    0.999999999872559,
    -0.12499999898030063,
    0.002604165343651872,
    -2.170076051907257e-05,
    9.674607230271745e-08,
    -2.5566742521071554e-10,
)


def polynomial(terms, z):
    total = terms[-1] * z + terms[-2]
    for term in terms[-3::-1]:
        total = total * z + term
    return total


def half_angle(field):
    z = field * field
    return field * polynomial(SINE, z), polynomial(COSINE, z)


def pack(block):
    rows, width = block.shape
    if not packs(rows, width):
        return (block,)
    full = width - LANES // 2
    tail = jnp.concatenate([block[: rows // 2, full:], block[rows // 2 :, full:]], 1)
    return tuple(block[:, i : i + LANES] for i in range(0, full, LANES)) + (tail,)


def packs(rows, width):
    return width > LANES and width % LANES == LANES // 2 and rows % 16 == 0


def packed_shape(rows, width):
    return (rows * width // LANES, LANES) if packs(rows, width) else (rows, width)


def unpack(block, rows, width):
    if not packs(rows, width):
        return block
    full = width - LANES // 2
    count = full // LANES
    pieces = [block[i * rows : (i + 1) * rows] for i in range(count)]
    tail = block[count * rows :]
    pieces.append(jnp.concatenate([tail[:, : LANES // 2], tail[:, LANES // 2 :]], 0))
    return jnp.concatenate(pieces, 1)


def local_kernel(
    seg_total,
    coil_total,
    count_ref,
    time_hbm,
    rows_hbm,
    fourier_hbm,
    cols_hbm,
    field_hbm,
    maps_hbm,
    image_hbm,
    measured_hbm,
    kept_ref,
    away_ref,
    own_ref,
    time_ref,
    rows_ref,
    fourier_ref,
    cols_ref,
    field_ref,
    maps_ref,
    image_ref,
    measured_ref,
    wave_ref,
    phase_ref,
    left_ref,
    right_ref,
    inner_ref,
    misfit_ref,
    row_ref,
    turned_ref,
    scaled_ref,
    back_ref,
    term_ref,
    sems,
):
    pixels = field_ref.shape[0]
    row_total = rows_hbm.shape[0]
    col_total = cols_hbm.shape[0]
    own_rows = row_total // seg_total
    width = 2 * pixels // seg_total
    pairs = seg_total // 2
    block_rows = pixels // coil_total
    groups = coil_total // 2
    cuts = [0] + [pixels * cut // 384 for cut in CUTS]
    segment = lax.axis_index("seg")
    member = lax.axis_index("coil")

    copies = [
        pltpu.make_async_copy(source, target, sems.at[i])
        for i, (source, target) in enumerate(
            (
                (field_hbm, field_ref),
                (cols_hbm, cols_ref),
                (fourier_hbm, fourier_ref),
                (rows_hbm, rows_ref),
                (time_hbm, time_ref),
                (image_hbm, image_ref),
                (maps_hbm, maps_ref),
                (measured_hbm, measured_ref),
            )
        )
    ]
    for copy in copies:
        copy.start()
    for copy in copies[:5]:
        copy.wait()

    def phases(first, last):
        for low in range(first, last, PIECE):
            rows = slice(low, low + PIECE)
            sine, cosine = half_angle(field_ref[rows, :])
            twice = 4.0 * (cosine * cosine) - 2.0
            previous = (cosine, -sine)
            for pair in range(pairs):
                if pair == 1:
                    previous, cosine, sine = (
                        (cosine, sine),
                        twice * cosine - cosine,
                        twice * sine + sine,
                    )
                elif pair:
                    previous, cosine, sine = (
                        (cosine, sine),
                        twice * cosine - previous[0],
                        twice * sine - previous[1],
                    )
                phase_ref[2 * pair, rows, :] = cosine
                phase_ref[2 * pair + 1, rows, :] = sine

    early = EARLY * pixels // 384 // PIECE * PIECE
    col_op = dot(cols_ref[...], fourier_ref[...]).astype(jnp.bfloat16)
    phases(0, early // 2 // PIECE * PIECE)
    left_ref[:col_total, :pixels] = col_op[:, :pixels]
    left_ref[:col_total, pixels:] = -col_op[:, pixels:]
    left_ref[col_total:, :pixels] = col_op[:, pixels:]
    left_ref[col_total:, pixels:] = col_op[:, :pixels]
    col_re = jnp.transpose(col_op[:, :pixels])
    col_im = jnp.transpose(col_op[:, pixels:])
    right_ref[:pixels, :col_total] = col_re
    right_ref[:pixels, col_total:] = col_im
    right_ref[pixels:, :col_total] = -col_im
    right_ref[pixels:, col_total:] = col_re
    row_op = dot(rows_ref[...], fourier_ref[...]).astype(jnp.bfloat16)
    row_ref[...] = row_op
    phases(early // 2 // PIECE * PIECE, early)

    steps = jnp.broadcast_to(time_ref[...].astype(jnp.float32), (8, row_total))

    def weight(s):
        return jnp.maximum(0.0, 1.0 - jnp.abs(steps - float(s * SUBSTEPS)) / SUBSTEPS)

    along = []
    for pair in range(pairs):
        above, below = weight(pairs + pair), weight(pairs - 1 - pair)
        along += [above + below, above - below]
    for copy in copies[5:]:
        copy.wait()
    for part in range(2):
        adjoint = jnp.transpose(row_op[:, part * pixels : (part + 1) * pixels])
        columns = slice(part * row_total, (part + 1) * row_total)
        for i in range(seg_total):
            scaled = adjoint * along[i][:1].astype(jnp.bfloat16)
            for first, last in zip(cuts, cuts[1:]):
                base = first * seg_total + i * (last - first)
                scaled_ref[base : base + last - first, columns] = scaled[first:last]

    right = right_ref[...]
    for chunk in range(pixels // CHUNK):
        phases(max(early, chunk * CHUNK), max(early, (chunk + 1) * CHUNK))
        for low in range(0, CHUNK, PIECE):
            rows = slice(chunk * CHUNK + low, chunk * CHUNK + low + PIECE)
            image_re, image_im = image_ref[rows, :pixels], image_ref[rows, pixels:]
            map_re, map_im = maps_ref[rows, :pixels], maps_ref[rows, pixels:]
            base_re = image_re * map_re - image_im * map_im
            base_im = image_re * map_im + image_im * map_re
            for pair in range(pairs):
                cosine = phase_ref[2 * pair, rows, :].astype(jnp.bfloat16)
                sine = phase_ref[2 * pair + 1, rows, :].astype(jnp.bfloat16)
                even = slice(2 * pair * CHUNK + low, 2 * pair * CHUNK + low + PIECE)
                odd = slice(even.start + CHUNK, even.stop + CHUNK)
                wave_ref[chunk, even, :pixels] = base_re * cosine
                wave_ref[chunk, even, pixels:] = base_im * cosine
                wave_ref[chunk, odd, :pixels] = -base_im * sine
                wave_ref[chunk, odd, pixels:] = base_re * sine
        v = dot(wave_ref[chunk], right).astype(jnp.bfloat16)
        for i in range(seg_total):
            piece = v[i * CHUNK : (i + 1) * CHUNK]
            first = slice(chunk * CHUNK, (chunk + 1) * CHUNK)
            second = slice(pixels + first.start, pixels + first.stop)
            lanes = i % 2 * 2 * col_total
            middle, end = lanes + col_total, lanes + 2 * col_total
            inner_ref[i // 2, first, lanes:end] = piece
            inner_ref[i // 2, second, lanes:middle] = -piece[:, col_total:]
            inner_ref[i // 2, second, middle:end] = piece[:, :col_total]
    samples = None
    for pair in range(pairs):
        y = dot(row_ref[...], inner_ref[pair])
        for i in range(2):
            part = y[:, i * 2 * col_total : (i + 1) * 2 * col_total]
            part = part * jnp.transpose(along[2 * pair + i])[:, :1]
            samples = part if samples is None else samples + part

    row_ids = lax.broadcasted_iota(jnp.int32, (row_total, 2 * col_total), 0)
    misfit = samples - measured_ref[...].astype(jnp.float32)
    misfit = jnp.where(row_ids < count_ref[0], misfit, 0.0)
    misfit_ref[...] = misfit
    own_start = pl.multiple_of(segment * own_rows, own_rows)
    own_ref[...] = misfit_ref[pl.ds(own_start, own_rows), :]

    column = lax.rem(segment * width, pixels)
    imaginary = segment * width >= pixels
    start = jnp.minimum(column // LANES * LANES, pixels - WINDOW)
    start = pl.multiple_of(start, LANES)
    after = pl.multiple_of(start + pixels, LANES)
    shift = lax.rem(WINDOW - (column - start), WINDOW)
    misfit = misfit.astype(jnp.bfloat16)
    turn_re = dot(misfit, left_ref[:, pl.ds(start, WINDOW)]).astype(jnp.bfloat16)
    turn_im = dot(misfit, left_ref[:, pl.ds(after, WINDOW)]).astype(jnp.bfloat16)
    turned_ref[:row_total, :WINDOW] = turn_re
    turned_ref[:row_total, WINDOW:] = turn_im
    turned_ref[row_total:, :WINDOW] = turn_im
    turned_ref[row_total:, WINDOW:] = -turn_re
    turned = turned_ref[...]
    factor = coil_total ** (-0.5)
    for first, last in zip(cuts, cuts[1:]):
        tall = last - first
        part = slice(first * seg_total, last * seg_total)
        back_ref[part, :] = dot(scaled_ref[part, :], turned)
        for low in range(0, tall, PIECE):
            rows = slice(first + low, first + low + PIECE)
            sum_re = None
            for pair in range(pairs):
                cosine = phase_ref[2 * pair, rows, pl.ds(start, WINDOW)]
                sine = phase_ref[2 * pair + 1, rows, pl.ds(start, WINDOW)]
                base = first * seg_total + 2 * pair * tall + low
                even = slice(base, base + PIECE)
                odd = slice(base + tall, base + tall + PIECE)
                add_re = cosine * back_ref[even, :WINDOW]
                add_re = add_re + sine * back_ref[odd, WINDOW:]
                add_im = cosine * back_ref[even, WINDOW:]
                add_im = add_im - sine * back_ref[odd, :WINDOW]
                sum_re = add_re if sum_re is None else sum_re + add_re
                sum_im = add_im if pair == 0 else sum_im + add_im
            map_re = maps_ref[rows, pl.ds(start, WINDOW)].astype(jnp.float32)
            map_im = maps_ref[rows, pl.ds(after, WINDOW)].astype(jnp.float32)
            for_re = jnp.where(imaginary, -map_im, map_re) * factor
            for_im = jnp.where(imaginary, map_re, map_im) * factor
            term_ref[rows, :] = pltpu.roll(for_re * sum_re + for_im * sum_im, shift, 1)

    lane = lax.rem(member, 2)
    group = member // 2
    for g in range(groups):
        slot = slot_of(g, group, groups)
        upper = term_ref[2 * g * block_rows : (2 * g + 1) * block_rows, :width]
        lower = term_ref[(2 * g + 1) * block_rows : (2 * g + 2) * block_rows, :width]
        for ref, value in (
            (kept_ref, jnp.where(lane == 0, upper, lower)),
            (away_ref, jnp.where(lane == 0, lower, upper)),
        ):
            top = 0
            for piece in pack(value):
                ref[slot, top : top + piece.shape[0], :] = piece
                top += piece.shape[0]


def local_terms(seg_total, coil_total, image, maps, field, rows, cols, measured, time, count):
    pixels = field.shape[0]
    row_total, col_total = rows.shape[0], cols.shape[0]
    width = 2 * pixels // seg_total
    fourier = jnp.asarray(dft_tables(pixels), jnp.bfloat16)
    anywhere = pl.BlockSpec(memory_space=pl.ANY)
    vmem = pl.BlockSpec(memory_space=pltpu.VMEM)
    smem = pl.BlockSpec(memory_space=pltpu.SMEM)
    operands = (time, rows, fourier, cols, field, maps, image, measured)
    blocks = (coil_total // 2, *packed_shape(pixels // coil_total, width))
    return pl.pallas_call(
        functools.partial(local_kernel, seg_total, coil_total),
        out_shape=(
            pltpu.VMEM(blocks, jnp.float32),
            pltpu.VMEM(blocks, jnp.float32),
            pltpu.VMEM((row_total // seg_total, 2 * col_total), jnp.float32),
        ),
        in_specs=[smem] + [anywhere] * len(operands),
        out_specs=(vmem, vmem, vmem),
        scratch_shapes=[pltpu.VMEM(x.shape, x.dtype) for x in operands]
        + [
            pltpu.VMEM((pixels // CHUNK, seg_total * CHUNK, 2 * pixels), jnp.bfloat16),
            pltpu.VMEM((seg_total, pixels, pixels), jnp.float32),
            pltpu.VMEM((2 * col_total, 2 * pixels), jnp.bfloat16),
            pltpu.VMEM((2 * pixels, 2 * col_total), jnp.bfloat16),
            pltpu.VMEM((seg_total // 2, 2 * pixels, 4 * col_total), jnp.bfloat16),
            pltpu.VMEM((row_total, 2 * col_total), jnp.float32),
            pltpu.VMEM((row_total, 2 * pixels), jnp.bfloat16),
            pltpu.VMEM((2 * row_total, 2 * WINDOW), jnp.bfloat16),
            pltpu.VMEM((seg_total * pixels, 2 * row_total), jnp.bfloat16),
            pltpu.VMEM((seg_total * pixels, 2 * WINDOW), jnp.float32),
            pltpu.VMEM((pixels, WINDOW), jnp.float32),
            pltpu.SemaphoreType.DMA((8,)),
        ],
        compiler_params=pltpu.CompilerParams(vmem_limit_bytes=56 * 1024 * 1024),
        name="local_terms",
    )(count, *operands)


def routes(groups):
    if groups == 4:
        return [(2, 3, 1, 0), (3, 2, 0, 1), (1, 0, 3, 2)]
    return [tuple((z + step) % groups for z in range(groups)) for step in range(1, groups)]


def slot_of(target, group, groups):
    if groups != 4:
        return lax.rem(target + groups - group, groups)
    slot = jnp.int32(0)
    for k, route in enumerate(routes(groups)):
        slot = jnp.where(group == route.index(target), k + 1, slot)
    return slot


def exchange_sum(kept, away, axis):
    total = lax.axis_size(axis)
    paired = kept + lax.ppermute(away, axis, [(i, i ^ 1) for i in range(total)])
    result = paired[0]
    for k, route in enumerate(routes(total // 2)):
        pairs = [(i, 2 * route[i // 2] + i % 2) for i in range(total)]
        got = lax.ppermute(paired[k + 1], axis, pairs)
        result = result + got
    return result


def shards(
    image_estimate,
    coil_maps,
    field_map,
    interp_rows,
    interp_cols,
    measured,
    sample_time,
    sample_count,
):
    seg_total = lax.axis_size("seg")
    coil_total = lax.axis_size("coil")
    pixels = field_map.shape[0]
    kept, away, own = local_terms(
        seg_total,
        coil_total,
        image_estimate[0],
        coil_maps[0],
        field_map,
        interp_rows[0],
        interp_cols[0],
        measured[0, 0],
        sample_time,
        sample_count,
    )
    total = exchange_sum(kept, away, "coil")
    gradient = unpack(total, pixels // coil_total, 2 * pixels // seg_total)
    return gradient[None], own[None, None]


def solution(mesh):
    in_specs = (P(), P("coil", None, None), P(), P(), P(), P("coil", None, None, None), P(), P())
    out_specs = (P(None, "coil", "seg"), P("coil", None, "seg", None))
    return jax.shard_map(
        shards, mesh=mesh, in_specs=in_specs, out_specs=out_specs, check_vma=False
    )
```

```python
import functools
import math

import jax
import jax.numpy as jnp
import numpy as np
from jax import lax
from jax.experimental import pallas as pl
from jax.experimental.pallas import tpu as pltpu
from jax.sharding import PartitionSpec as P

SUBSTEPS = 4
LANES = 128
WINDOW = 256
CHUNK = 192
EARLY = 192
CUTS = (192, 384)
PIECE = 16


def dft_tables(length):
    wrapped = np.outer(np.arange(length), np.arange(length)) % length
    angles = wrapped * (2.0 * math.pi / length)
    factor = 1.0 / math.sqrt(length)
    return np.concatenate([np.cos(angles) * factor, -np.sin(angles) * factor], 1)


def dot(a, b, contract=((1,), (0,))):
    return lax.dot_general(a, b, (contract, ((), ())), preferred_element_type=jnp.float32)


SINE = (
    0.49999999863922073,
    -0.020833325771248395,
    0.00026040993453922765,
    -1.5479976876565651e-06,
    5.113416832465264e-09,
)
COSINE = (
    0.9999999702593707,
    -0.12499983471729101,
    0.002604019482658158,
    -2.1655414954854096e-05,
    9.099108440040481e-08,
)


def polynomial(terms, z):
    total = terms[-1] * z + terms[-2]
    for term in terms[-3::-1]:
        total = total * z + term
    return total


def half_angle(field):
    z = field * field
    return field * polynomial(SINE, z), polynomial(COSINE, z)


def pack(block):
    rows, width = block.shape
    if not packs(rows, width):
        return (block,)
    full = width - LANES // 2
    tail = jnp.concatenate([block[: rows // 2, full:], block[rows // 2 :, full:]], 1)
    return tuple(block[:, i : i + LANES] for i in range(0, full, LANES)) + (tail,)


def packs(rows, width):
    return width > LANES and width % LANES == LANES // 2 and rows % 16 == 0


def packed_shape(rows, width):
    return (rows * width // LANES, LANES) if packs(rows, width) else (rows, width)


def unpack(block, rows, width):
    if not packs(rows, width):
        return block
    full = width - LANES // 2
    count = full // LANES
    pieces = [block[i * rows : (i + 1) * rows] for i in range(count)]
    tail = block[count * rows :]
    pieces.append(jnp.concatenate([tail[:, : LANES // 2], tail[:, LANES // 2 :]], 0))
    return jnp.concatenate(pieces, 1)


def local_kernel(
    seg_total,
    coil_total,
    count_ref,
    time_hbm,
    rows_hbm,
    fourier_hbm,
    cols_hbm,
    field_hbm,
    maps_hbm,
    image_hbm,
    measured_hbm,
    kept_ref,
    away_ref,
    own_ref,
    time_ref,
    rows_ref,
    fourier_ref,
    cols_ref,
    field_ref,
    maps_ref,
    image_ref,
    measured_ref,
    wave_ref,
    phase_ref,
    left_ref,
    right_ref,
    inner_ref,
    misfit_ref,
    row_ref,
    turned_ref,
    scaled_ref,
    back_ref,
    term_ref,
    sems,
):
    pixels = field_ref.shape[0]
    row_total = rows_hbm.shape[0]
    col_total = cols_hbm.shape[0]
    own_rows = row_total // seg_total
    width = 2 * pixels // seg_total
    pairs = seg_total // 2
    block_rows = pixels // coil_total
    groups = coil_total // 2
    cuts = [0] + [pixels * cut // 384 for cut in CUTS]
    segment = lax.axis_index("seg")
    member = lax.axis_index("coil")

    copies = [
        pltpu.make_async_copy(source, target, sems.at[i])
        for i, (source, target) in enumerate(
            (
                (field_hbm, field_ref),
                (cols_hbm, cols_ref),
                (fourier_hbm, fourier_ref),
                (rows_hbm, rows_ref),
                (time_hbm, time_ref),
                (image_hbm, image_ref),
                (maps_hbm, maps_ref),
                (measured_hbm, measured_ref),
            )
        )
    ]
    for copy in copies:
        copy.start()
    for copy in copies[:5]:
        copy.wait()

    def phases(first, last):
        for low in range(first, last, PIECE):
            rows = slice(low, low + PIECE)
            sine, cosine = half_angle(field_ref[rows, :])
            twice = 4.0 * (cosine * cosine) - 2.0
            previous = (cosine, -sine)
            for pair in range(pairs):
                if pair == 1:
                    previous, cosine, sine = (
                        (cosine, sine),
                        twice * cosine - cosine,
                        twice * sine + sine,
                    )
                elif pair:
                    previous, cosine, sine = (
                        (cosine, sine),
                        twice * cosine - previous[0],
                        twice * sine - previous[1],
                    )
                phase_ref[2 * pair, rows, :] = cosine
                phase_ref[2 * pair + 1, rows, :] = sine

    early = EARLY * pixels // 384 // PIECE * PIECE
    col_op = dot(cols_ref[...], fourier_ref[...]).astype(jnp.bfloat16)
    phases(0, early // 2 // PIECE * PIECE)
    left_ref[:col_total, :pixels] = col_op[:, :pixels]
    left_ref[:col_total, pixels:] = -col_op[:, pixels:]
    left_ref[col_total:, :pixels] = col_op[:, pixels:]
    left_ref[col_total:, pixels:] = col_op[:, :pixels]
    col_re = jnp.transpose(col_op[:, :pixels])
    col_im = jnp.transpose(col_op[:, pixels:])
    right_ref[:pixels, :col_total] = col_re
    right_ref[:pixels, col_total:] = col_im
    right_ref[pixels:, :col_total] = -col_im
    right_ref[pixels:, col_total:] = col_re
    row_op = dot(rows_ref[...], fourier_ref[...]).astype(jnp.bfloat16)
    row_ref[...] = row_op
    phases(early // 2 // PIECE * PIECE, early)

    steps = jnp.broadcast_to(time_ref[...].astype(jnp.float32), (8, row_total))

    def weight(s):
        return jnp.maximum(0.0, 1.0 - jnp.abs(steps - float(s * SUBSTEPS)) / SUBSTEPS)

    along = []
    for pair in range(pairs):
        above, below = weight(pairs + pair), weight(pairs - 1 - pair)
        along += [above + below, above - below]
    for copy in copies[5:]:
        copy.wait()
    for part in range(2):
        adjoint = jnp.transpose(row_op[:, part * pixels : (part + 1) * pixels])
        columns = slice(part * row_total, (part + 1) * row_total)
        for i in range(seg_total):
            scaled = adjoint * along[i][:1].astype(jnp.bfloat16)
            for first, last in zip(cuts, cuts[1:]):
                base = first * seg_total + i * (last - first)
                scaled_ref[base : base + last - first, columns] = scaled[first:last]

    right = right_ref[...]
    for chunk in range(pixels // CHUNK):
        phases(max(early, chunk * CHUNK), max(early, (chunk + 1) * CHUNK))
        for low in range(0, CHUNK, PIECE):
            rows = slice(chunk * CHUNK + low, chunk * CHUNK + low + PIECE)
            image_re, image_im = image_ref[rows, :pixels], image_ref[rows, pixels:]
            map_re, map_im = maps_ref[rows, :pixels], maps_ref[rows, pixels:]
            base_re = image_re * map_re - image_im * map_im
            base_im = image_re * map_im + image_im * map_re
            for pair in range(pairs):
                cosine = phase_ref[2 * pair, rows, :].astype(jnp.bfloat16)
                sine = phase_ref[2 * pair + 1, rows, :].astype(jnp.bfloat16)
                even = slice(2 * pair * CHUNK + low, 2 * pair * CHUNK + low + PIECE)
                odd = slice(even.start + CHUNK, even.stop + CHUNK)
                wave_ref[chunk, even, :pixels] = base_re * cosine
                wave_ref[chunk, even, pixels:] = base_im * cosine
                wave_ref[chunk, odd, :pixels] = -base_im * sine
                wave_ref[chunk, odd, pixels:] = base_re * sine
        v = dot(wave_ref[chunk], right).astype(jnp.bfloat16)
        for i in range(seg_total):
            piece = v[i * CHUNK : (i + 1) * CHUNK]
            first = slice(chunk * CHUNK, (chunk + 1) * CHUNK)
            second = slice(pixels + first.start, pixels + first.stop)
            lanes = i % 2 * 2 * col_total
            middle, end = lanes + col_total, lanes + 2 * col_total
            inner_ref[i // 2, first, lanes:end] = piece
            inner_ref[i // 2, second, lanes:middle] = -piece[:, col_total:]
            inner_ref[i // 2, second, middle:end] = piece[:, :col_total]
    samples = None
    for pair in range(pairs):
        y = dot(row_ref[...], inner_ref[pair])
        for i in range(2):
            part = y[:, i * 2 * col_total : (i + 1) * 2 * col_total]
            part = part * jnp.transpose(along[2 * pair + i])[:, :1]
            samples = part if samples is None else samples + part

    row_ids = lax.broadcasted_iota(jnp.int32, (row_total, 2 * col_total), 0)
    misfit = samples - measured_ref[...].astype(jnp.float32)
    misfit = jnp.where(row_ids < count_ref[0], misfit, 0.0)
    misfit_ref[...] = misfit
    own_start = pl.multiple_of(segment * own_rows, own_rows)
    own_ref[...] = misfit_ref[pl.ds(own_start, own_rows), :]

    column = lax.rem(segment * width, pixels)
    imaginary = segment * width >= pixels
    start = jnp.minimum(column // LANES * LANES, pixels - WINDOW)
    start = pl.multiple_of(start, LANES)
    after = pl.multiple_of(start + pixels, LANES)
    shift = lax.rem(WINDOW - (column - start), WINDOW)
    misfit = misfit.astype(jnp.bfloat16)
    turn_re = dot(misfit, left_ref[:, pl.ds(start, WINDOW)]).astype(jnp.bfloat16)
    turn_im = dot(misfit, left_ref[:, pl.ds(after, WINDOW)]).astype(jnp.bfloat16)
    turned_ref[:row_total, :WINDOW] = turn_re
    turned_ref[:row_total, WINDOW:] = turn_im
    turned_ref[row_total:, :WINDOW] = turn_im
    turned_ref[row_total:, WINDOW:] = -turn_re
    turned = turned_ref[...]
    factor = coil_total ** (-0.5)
    for first, last in zip(cuts, cuts[1:]):
        tall = last - first
        part = slice(first * seg_total, last * seg_total)
        back_ref[part, :] = dot(scaled_ref[part, :], turned)
        for low in range(0, tall, PIECE):
            rows = slice(first + low, first + low + PIECE)
            sum_re = None
            for pair in range(pairs):
                cosine = phase_ref[2 * pair, rows, pl.ds(start, WINDOW)]
                sine = phase_ref[2 * pair + 1, rows, pl.ds(start, WINDOW)]
                base = first * seg_total + 2 * pair * tall + low
                even = slice(base, base + PIECE)
                odd = slice(base + tall, base + tall + PIECE)
                add_re = cosine * back_ref[even, :WINDOW]
                add_re = add_re + sine * back_ref[odd, WINDOW:]
                add_im = cosine * back_ref[even, WINDOW:]
                add_im = add_im - sine * back_ref[odd, :WINDOW]
                sum_re = add_re if sum_re is None else sum_re + add_re
                sum_im = add_im if pair == 0 else sum_im + add_im
            map_re = maps_ref[rows, pl.ds(start, WINDOW)].astype(jnp.float32)
            map_im = maps_ref[rows, pl.ds(after, WINDOW)].astype(jnp.float32)
            for_re = jnp.where(imaginary, -map_im, map_re) * factor
            for_im = jnp.where(imaginary, map_re, map_im) * factor
            term_ref[rows, :] = pltpu.roll(for_re * sum_re + for_im * sum_im, shift, 1)

    lane = lax.rem(member, 2)
    group = member // 2
    for g in range(groups):
        slot = slot_of(g, group, groups)
        upper = term_ref[2 * g * block_rows : (2 * g + 1) * block_rows, :width]
        lower = term_ref[(2 * g + 1) * block_rows : (2 * g + 2) * block_rows, :width]
        for ref, value in (
            (kept_ref, jnp.where(lane == 0, upper, lower)),
            (away_ref, jnp.where(lane == 0, lower, upper)),
        ):
            top = 0
            for piece in pack(value):
                ref[slot, top : top + piece.shape[0], :] = piece
                top += piece.shape[0]


def local_terms(seg_total, coil_total, image, maps, field, rows, cols, measured, time, count):
    pixels = field.shape[0]
    row_total, col_total = rows.shape[0], cols.shape[0]
    width = 2 * pixels // seg_total
    fourier = jnp.asarray(dft_tables(pixels), jnp.bfloat16)
    anywhere = pl.BlockSpec(memory_space=pl.ANY)
    vmem = pl.BlockSpec(memory_space=pltpu.VMEM)
    smem = pl.BlockSpec(memory_space=pltpu.SMEM)
    operands = (time, rows, fourier, cols, field, maps, image, measured)
    blocks = (coil_total // 2, *packed_shape(pixels // coil_total, width))
    return pl.pallas_call(
        functools.partial(local_kernel, seg_total, coil_total),
        out_shape=(
            pltpu.VMEM(blocks, jnp.float32),
            pltpu.VMEM(blocks, jnp.float32),
            pltpu.VMEM((row_total // seg_total, 2 * col_total), jnp.float32),
        ),
        in_specs=[smem] + [anywhere] * len(operands),
        out_specs=(vmem, vmem, vmem),
        scratch_shapes=[pltpu.VMEM(x.shape, x.dtype) for x in operands]
        + [
            pltpu.VMEM((pixels // CHUNK, seg_total * CHUNK, 2 * pixels), jnp.bfloat16),
            pltpu.VMEM((seg_total, pixels, pixels), jnp.float32),
            pltpu.VMEM((2 * col_total, 2 * pixels), jnp.bfloat16),
            pltpu.VMEM((2 * pixels, 2 * col_total), jnp.bfloat16),
            pltpu.VMEM((seg_total // 2, 2 * pixels, 4 * col_total), jnp.bfloat16),
            pltpu.VMEM((row_total, 2 * col_total), jnp.float32),
            pltpu.VMEM((row_total, 2 * pixels), jnp.bfloat16),
            pltpu.VMEM((2 * row_total, 2 * WINDOW), jnp.bfloat16),
            pltpu.VMEM((seg_total * pixels, 2 * row_total), jnp.bfloat16),
            pltpu.VMEM((seg_total * pixels, 2 * WINDOW), jnp.float32),
            pltpu.VMEM((pixels, WINDOW), jnp.float32),
            pltpu.SemaphoreType.DMA((8,)),
        ],
        compiler_params=pltpu.CompilerParams(vmem_limit_bytes=56 * 1024 * 1024),
        name="local_terms",
    )(count, *operands)


def routes(groups):
    if groups == 4:
        return [(1, 2, 3, 0), (2, 3, 0, 1), (3, 0, 1, 2)]
    return [tuple((z + step) % groups for z in range(groups)) for step in range(1, groups)]


def slot_of(target, group, groups):
    slot = jnp.int32(groups - 1)
    if groups != 4:
        return lax.rem(target + 2 * groups - 1 - group, groups)
    for k, route in enumerate(routes(groups)):
        slot = jnp.where(group == route.index(target), k, slot)
    return slot


def exchange_sum(kept, away, axis):
    total = lax.axis_size(axis)
    last = total // 2 - 1
    swap = [(i, i ^ 1) for i in range(total)]
    plan = [[(i, 2 * route[i // 2] + i % 2) for i in range(total)] for route in routes(total // 2)]
    got = lax.ppermute(away[1:last], axis, swap)
    both = lax.ppermute(jnp.stack([kept[0], away[0]]), axis, plan[0])
    paired = kept[1:last] + got
    result = kept[last] + both[0]
    for k in range(1, last):
        got = lax.ppermute(paired[k - 1], axis, plan[k])
        result = result + got
    got = lax.ppermute(away[last] + both[1], axis, swap)
    return result + got


def shards(
    image_estimate,
    coil_maps,
    field_map,
    interp_rows,
    interp_cols,
    measured,
    sample_time,
    sample_count,
):
    seg_total = lax.axis_size("seg")
    coil_total = lax.axis_size("coil")
    pixels = field_map.shape[0]
    kept, away, own = local_terms(
        seg_total,
        coil_total,
        image_estimate[0],
        coil_maps[0],
        field_map,
        interp_rows[0],
        interp_cols[0],
        measured[0, 0],
        sample_time,
        sample_count,
    )
    total = exchange_sum(kept, away, "coil")
    gradient = unpack(total, pixels // coil_total, 2 * pixels // seg_total)
    return gradient[None], own[None, None]


def solution(mesh):
    in_specs = (P(), P("coil", None, None), P(), P(), P(), P("coil", None, None, None), P(), P())
    out_specs = (P(None, "coil", "seg"), P("coil", None, "seg", None))
    return jax.shard_map(
        shards, mesh=mesh, in_specs=in_specs, out_specs=out_specs, check_vma=False
    )
```

```python
import functools
import math

import jax
import jax.numpy as jnp
import numpy as np
from jax import lax
from jax.experimental import pallas as pl
from jax.experimental.pallas import tpu as pltpu
from jax.sharding import PartitionSpec as P

SUBSTEPS = 4
LANES = 128
WINDOW = 256
CHUNK = 192
EARLY = 384
ZERO = 192
CUTS = (192, 384)
PIECE = 16


def dft_tables(length):
    wrapped = np.outer(np.arange(length), np.arange(length)) % length
    angles = wrapped * (2.0 * math.pi / length)
    factor = 1.0 / math.sqrt(length)
    return np.concatenate([np.cos(angles) * factor, -np.sin(angles) * factor], 1)


def dot(a, b, contract=((1,), (0,))):
    return lax.dot_general(a, b, (contract, ((), ())), preferred_element_type=jnp.float32)


SINE = (
    0.49999999863922073,
    -0.020833325771248395,
    0.00026040993453922765,
    -1.5479976876565651e-06,
    5.113416832465264e-09,
)
COSINE = (
    0.9999999702593707,
    -0.12499983471729101,
    0.002604019482658158,
    -2.1655414954854096e-05,
    9.099108440040481e-08,
)


def polynomial(terms, z):
    total = terms[-1] * z + terms[-2]
    for term in terms[-3::-1]:
        total = total * z + term
    return total


def half_angle(field):
    z = field * field
    return field * polynomial(SINE, z), polynomial(COSINE, z)


def pack(block):
    rows, width = block.shape
    if not packs(rows, width):
        return (block,)
    full = width - LANES // 2
    tail = jnp.concatenate([block[: rows // 2, full:], block[rows // 2 :, full:]], 1)
    return tuple(block[:, i : i + LANES] for i in range(0, full, LANES)) + (tail,)


def packs(rows, width):
    return width > LANES and width % LANES == LANES // 2 and rows % 16 == 0


def packed_shape(rows, width):
    return (rows * width // LANES, LANES) if packs(rows, width) else (rows, width)


def unpack(block, rows, width):
    if not packs(rows, width):
        return block
    full = width - LANES // 2
    count = full // LANES
    pieces = [block[i * rows : (i + 1) * rows] for i in range(count)]
    tail = block[count * rows :]
    pieces.append(jnp.concatenate([tail[:, : LANES // 2], tail[:, LANES // 2 :]], 0))
    return jnp.concatenate(pieces, 1)


def local_kernel(
    seg_total,
    coil_total,
    count_ref,
    time_hbm,
    rows_hbm,
    fourier_hbm,
    cols_hbm,
    field_hbm,
    maps_hbm,
    image_hbm,
    measured_hbm,
    kept_ref,
    away_ref,
    own_ref,
    time_ref,
    rows_ref,
    fourier_ref,
    cols_ref,
    field_ref,
    maps_ref,
    image_ref,
    measured_ref,
    wave_ref,
    phase_ref,
    left_ref,
    right_ref,
    inner_ref,
    misfit_ref,
    row_ref,
    turned_ref,
    scaled_ref,
    back_ref,
    term_ref,
    sems,
):
    pixels = field_ref.shape[0]
    row_total = rows_hbm.shape[0]
    col_total = cols_hbm.shape[0]
    own_rows = row_total // seg_total
    width = 2 * pixels // seg_total
    pairs = seg_total // 2
    block_rows = pixels // coil_total
    groups = coil_total // 2
    cuts = [0] + [pixels * cut // 384 for cut in CUTS]
    segment = lax.axis_index("seg")
    member = lax.axis_index("coil")

    copies = [
        pltpu.make_async_copy(source, target, sems.at[i])
        for i, (source, target) in enumerate(
            (
                (field_hbm, field_ref),
                (cols_hbm, cols_ref),
                (fourier_hbm, fourier_ref),
                (rows_hbm, rows_ref),
                (time_hbm, time_ref),
                (image_hbm, image_ref),
                (maps_hbm, maps_ref),
                (measured_hbm, measured_ref),
            )
        )
    ]
    for copy in copies:
        copy.start()
    copies[0].wait()

    def phases(first, last):
        for low in range(first, last, PIECE):
            rows = slice(low, low + PIECE)
            sine, cosine = half_angle(field_ref[rows, :])
            twice = 4.0 * (cosine * cosine) - 2.0
            previous = (cosine, -sine)
            for pair in range(pairs):
                if pair == 1:
                    previous, cosine, sine = (
                        (cosine, sine),
                        twice * cosine - cosine,
                        twice * sine + sine,
                    )
                elif pair:
                    previous, cosine, sine = (
                        (cosine, sine),
                        twice * cosine - previous[0],
                        twice * sine - previous[1],
                    )
                phase_ref[2 * pair, rows, :] = cosine
                phase_ref[2 * pair + 1, rows, :] = sine

    first_rows = ZERO * pixels // 384 // PIECE * PIECE
    phases(0, first_rows)
    for copy in copies[1:5]:
        copy.wait()
    early = EARLY * pixels // 384 // PIECE * PIECE
    col_op = dot(cols_ref[...], fourier_ref[...]).astype(jnp.bfloat16)
    phases(first_rows, early)
    left_ref[:col_total, :pixels] = col_op[:, :pixels]
    left_ref[:col_total, pixels:] = -col_op[:, pixels:]
    left_ref[col_total:, :pixels] = col_op[:, pixels:]
    left_ref[col_total:, pixels:] = col_op[:, :pixels]
    col_re = jnp.transpose(col_op[:, :pixels])
    col_im = jnp.transpose(col_op[:, pixels:])
    right_ref[:pixels, :col_total] = col_re
    right_ref[:pixels, col_total:] = col_im
    right_ref[pixels:, :col_total] = -col_im
    right_ref[pixels:, col_total:] = col_re
    row_op = dot(rows_ref[...], fourier_ref[...]).astype(jnp.bfloat16)
    row_ref[...] = row_op

    steps = jnp.broadcast_to(time_ref[...].astype(jnp.float32), (8, row_total))

    def weight(s):
        return jnp.maximum(0.0, 1.0 - jnp.abs(steps - float(s * SUBSTEPS)) / SUBSTEPS)

    along = []
    for pair in range(pairs):
        above, below = weight(pairs + pair), weight(pairs - 1 - pair)
        along += [above + below, above - below]
    for copy in copies[5:]:
        copy.wait()
    for part in range(2):
        adjoint = jnp.transpose(row_op[:, part * pixels : (part + 1) * pixels])
        columns = slice(part * row_total, (part + 1) * row_total)
        for i in range(seg_total):
            scaled = adjoint * along[i][:1].astype(jnp.bfloat16)
            for first, last in zip(cuts, cuts[1:]):
                base = first * seg_total + i * (last - first)
                scaled_ref[base : base + last - first, columns] = scaled[first:last]

    right = right_ref[...]
    for chunk in range(pixels // CHUNK):
        phases(max(early, chunk * CHUNK), max(early, (chunk + 1) * CHUNK))
        for low in range(0, CHUNK, PIECE):
            rows = slice(chunk * CHUNK + low, chunk * CHUNK + low + PIECE)
            image_re, image_im = image_ref[rows, :pixels], image_ref[rows, pixels:]
            map_re, map_im = maps_ref[rows, :pixels], maps_ref[rows, pixels:]
            base_re = image_re * map_re - image_im * map_im
            base_im = image_re * map_im + image_im * map_re
            for pair in range(pairs):
                cosine = phase_ref[2 * pair, rows, :].astype(jnp.bfloat16)
                sine = phase_ref[2 * pair + 1, rows, :].astype(jnp.bfloat16)
                even = slice(2 * pair * CHUNK + low, 2 * pair * CHUNK + low + PIECE)
                odd = slice(even.start + CHUNK, even.stop + CHUNK)
                wave_ref[chunk, even, :pixels] = base_re * cosine
                wave_ref[chunk, even, pixels:] = base_im * cosine
                wave_ref[chunk, odd, :pixels] = -base_im * sine
                wave_ref[chunk, odd, pixels:] = base_re * sine
        v = dot(wave_ref[chunk], right).astype(jnp.bfloat16)
        for i in range(seg_total):
            piece = v[i * CHUNK : (i + 1) * CHUNK]
            first = slice(chunk * CHUNK, (chunk + 1) * CHUNK)
            second = slice(pixels + first.start, pixels + first.stop)
            lanes = i % 2 * 2 * col_total
            middle, end = lanes + col_total, lanes + 2 * col_total
            inner_ref[i // 2, first, lanes:end] = piece
            inner_ref[i // 2, second, lanes:middle] = -piece[:, col_total:]
            inner_ref[i // 2, second, middle:end] = piece[:, :col_total]
    samples = None
    for pair in range(pairs):
        y = dot(row_ref[...], inner_ref[pair])
        for i in range(2):
            part = y[:, i * 2 * col_total : (i + 1) * 2 * col_total]
            part = part * jnp.transpose(along[2 * pair + i])[:, :1]
            samples = part if samples is None else samples + part

    row_ids = lax.broadcasted_iota(jnp.int32, (row_total, 2 * col_total), 0)
    misfit = samples - measured_ref[...].astype(jnp.float32)
    misfit = jnp.where(row_ids < count_ref[0], misfit, 0.0)
    misfit_ref[...] = misfit
    own_start = pl.multiple_of(segment * own_rows, own_rows)
    own_ref[...] = misfit_ref[pl.ds(own_start, own_rows), :]

    column = lax.rem(segment * width, pixels)
    imaginary = segment * width >= pixels
    start = jnp.minimum(column // LANES * LANES, pixels - WINDOW)
    start = pl.multiple_of(start, LANES)
    after = pl.multiple_of(start + pixels, LANES)
    shift = lax.rem(WINDOW - (column - start), WINDOW)
    misfit = misfit.astype(jnp.bfloat16)
    turn_re = dot(misfit, left_ref[:, pl.ds(start, WINDOW)]).astype(jnp.bfloat16)
    turn_im = dot(misfit, left_ref[:, pl.ds(after, WINDOW)]).astype(jnp.bfloat16)
    turned_ref[:row_total, :WINDOW] = turn_re
    turned_ref[:row_total, WINDOW:] = turn_im
    turned_ref[row_total:, :WINDOW] = turn_im
    turned_ref[row_total:, WINDOW:] = -turn_re
    turned = turned_ref[...]
    factor = coil_total ** (-0.5)
    for first, last in zip(cuts, cuts[1:]):
        tall = last - first
        part = slice(first * seg_total, last * seg_total)
        back_ref[part, :] = dot(scaled_ref[part, :], turned)
        for low in range(0, tall, PIECE):
            rows = slice(first + low, first + low + PIECE)
            sum_re = None
            for pair in range(pairs):
                cosine = phase_ref[2 * pair, rows, pl.ds(start, WINDOW)]
                sine = phase_ref[2 * pair + 1, rows, pl.ds(start, WINDOW)]
                base = first * seg_total + 2 * pair * tall + low
                even = slice(base, base + PIECE)
                odd = slice(base + tall, base + tall + PIECE)
                add_re = cosine * back_ref[even, :WINDOW]
                add_re = add_re + sine * back_ref[odd, WINDOW:]
                add_im = cosine * back_ref[even, WINDOW:]
                add_im = add_im - sine * back_ref[odd, :WINDOW]
                sum_re = add_re if sum_re is None else sum_re + add_re
                sum_im = add_im if pair == 0 else sum_im + add_im
            map_re = maps_ref[rows, pl.ds(start, WINDOW)].astype(jnp.float32)
            map_im = maps_ref[rows, pl.ds(after, WINDOW)].astype(jnp.float32)
            for_re = jnp.where(imaginary, -map_im, map_re) * factor
            for_im = jnp.where(imaginary, map_re, map_im) * factor
            term_ref[rows, :] = pltpu.roll(for_re * sum_re + for_im * sum_im, shift, 1)

    lane = lax.rem(member, 2)
    group = member // 2
    for g in range(groups):
        slot = slot_of(g, group, groups)
        upper = term_ref[2 * g * block_rows : (2 * g + 1) * block_rows, :width]
        lower = term_ref[(2 * g + 1) * block_rows : (2 * g + 2) * block_rows, :width]
        for ref, value in (
            (kept_ref, jnp.where(lane == 0, upper, lower)),
            (away_ref, jnp.where(lane == 0, lower, upper)),
        ):
            top = 0
            for piece in pack(value):
                ref[slot, top : top + piece.shape[0], :] = piece
                top += piece.shape[0]


def local_terms(seg_total, coil_total, image, maps, field, rows, cols, measured, time, count):
    pixels = field.shape[0]
    row_total, col_total = rows.shape[0], cols.shape[0]
    width = 2 * pixels // seg_total
    fourier = jnp.asarray(dft_tables(pixels), jnp.bfloat16)
    anywhere = pl.BlockSpec(memory_space=pl.ANY)
    vmem = pl.BlockSpec(memory_space=pltpu.VMEM)
    smem = pl.BlockSpec(memory_space=pltpu.SMEM)
    operands = (time, rows, fourier, cols, field, maps, image, measured)
    blocks = (coil_total // 2, *packed_shape(pixels // coil_total, width))
    return pl.pallas_call(
        functools.partial(local_kernel, seg_total, coil_total),
        out_shape=(
            pltpu.VMEM(blocks, jnp.float32),
            pltpu.VMEM(blocks, jnp.float32),
            pltpu.VMEM((row_total // seg_total, 2 * col_total), jnp.float32),
        ),
        in_specs=[smem] + [anywhere] * len(operands),
        out_specs=(vmem, vmem, vmem),
        scratch_shapes=[pltpu.VMEM(x.shape, x.dtype) for x in operands]
        + [
            pltpu.VMEM((pixels // CHUNK, seg_total * CHUNK, 2 * pixels), jnp.bfloat16),
            pltpu.VMEM((seg_total, pixels, pixels), jnp.float32),
            pltpu.VMEM((2 * col_total, 2 * pixels), jnp.bfloat16),
            pltpu.VMEM((2 * pixels, 2 * col_total), jnp.bfloat16),
            pltpu.VMEM((seg_total // 2, 2 * pixels, 4 * col_total), jnp.bfloat16),
            pltpu.VMEM((row_total, 2 * col_total), jnp.float32),
            pltpu.VMEM((row_total, 2 * pixels), jnp.bfloat16),
            pltpu.VMEM((2 * row_total, 2 * WINDOW), jnp.bfloat16),
            pltpu.VMEM((seg_total * pixels, 2 * row_total), jnp.bfloat16),
            pltpu.VMEM((seg_total * pixels, 2 * WINDOW), jnp.float32),
            pltpu.VMEM((pixels, WINDOW), jnp.float32),
            pltpu.SemaphoreType.DMA((8,)),
        ],
        compiler_params=pltpu.CompilerParams(vmem_limit_bytes=56 * 1024 * 1024),
        name="local_terms",
    )(count, *operands)


def routes(groups):
    if groups == 4:
        return [(1, 2, 3, 0), (2, 3, 0, 1), (3, 0, 1, 2)]
    return [tuple((z + step) % groups for z in range(groups)) for step in range(1, groups)]


def slot_of(target, group, groups):
    slot = jnp.int32(groups - 1)
    if groups != 4:
        return lax.rem(target + 2 * groups - 1 - group, groups)
    for k, route in enumerate(routes(groups)):
        slot = jnp.where(group == route.index(target), k, slot)
    return slot


def exchange_sum(kept, away, axis):
    total = lax.axis_size(axis)
    last = total // 2 - 1
    swap = [(i, i ^ 1) for i in range(total)]
    plan = [[(i, 2 * route[i // 2] + i % 2) for i in range(total)] for route in routes(total // 2)]
    got = lax.ppermute(away[1:last], axis, swap)
    both = lax.ppermute(jnp.stack([kept[0], away[0]]), axis, plan[0])
    paired = kept[1:last] + got
    result = kept[last] + both[0]
    for k in range(1, last):
        got = lax.ppermute(paired[k - 1], axis, plan[k])
        result = result + got
    got = lax.ppermute(away[last] + both[1], axis, swap)
    return result + got


def shards(
    image_estimate,
    coil_maps,
    field_map,
    interp_rows,
    interp_cols,
    measured,
    sample_time,
    sample_count,
):
    seg_total = lax.axis_size("seg")
    coil_total = lax.axis_size("coil")
    pixels = field_map.shape[0]
    kept, away, own = local_terms(
        seg_total,
        coil_total,
        image_estimate[0],
        coil_maps[0],
        field_map,
        interp_rows[0],
        interp_cols[0],
        measured[0, 0],
        sample_time,
        sample_count,
    )
    total = exchange_sum(kept, away, "coil")
    gradient = unpack(total, pixels // coil_total, 2 * pixels // seg_total)
    return gradient[None], own[None, None]


def solution(mesh):
    in_specs = (P(), P("coil", None, None), P(), P(), P(), P("coil", None, None, None), P(), P())
    out_specs = (P(None, "coil", "seg"), P("coil", None, "seg", None))
    return jax.shard_map(
        shards, mesh=mesh, in_specs=in_specs, out_specs=out_specs, check_vma=False
    )
```

```python
import functools
import math

import jax
import jax.numpy as jnp
import numpy as np
from jax import lax
from jax.experimental import pallas as pl
from jax.experimental.pallas import tpu as pltpu
from jax.sharding import PartitionSpec as P

SUBSTEPS = 4
LANES = 128
WINDOW = 256
CHUNK = 192
EARLY = 384
ZERO = 192
CUTS = (48, 96, 144, 192)
PIECE = 16


def dft_tables(length):
    wrapped = np.outer(np.arange(length), np.arange(length)) % length
    angles = wrapped * (2.0 * math.pi / length)
    factor = 1.0 / math.sqrt(length)
    return np.concatenate([np.cos(angles) * factor, -np.sin(angles) * factor], 1)


def dot(a, b, contract=((1,), (0,))):
    return lax.dot_general(a, b, (contract, ((), ())), preferred_element_type=jnp.float32)


SINE = (
    0.49999999863922073,
    -0.020833325771248395,
    0.00026040993453922765,
    -1.5479976876565651e-06,
    5.113416832465264e-09,
)
COSINE = (
    0.9999999702593707,
    -0.12499983471729101,
    0.002604019482658158,
    -2.1655414954854096e-05,
    9.099108440040481e-08,
)


def polynomial(terms, z):
    total = terms[-1] * z + terms[-2]
    for term in terms[-3::-1]:
        total = total * z + term
    return total


def half_angle(field):
    z = field * field
    return field * polynomial(SINE, z), polynomial(COSINE, z)


def reverse_rows(block):
    order = 7 - lax.broadcasted_iota(jnp.int32, (8, LANES), 0)
    return jnp.concatenate(
        [
            jnp.concatenate(
                [
                    jnp.take_along_axis(block[i : i + 8, j : j + LANES], order, axis=0)
                    for j in range(0, block.shape[1], LANES)
                ],
                1,
            )
            for i in range(block.shape[0] - 8, -1, -8)
        ],
        0,
    )


def pack(block):
    rows, width = block.shape
    if not packs(rows, width):
        return (block,)
    full = width - LANES // 2
    tail = jnp.concatenate([block[: rows // 2, full:], block[rows // 2 :, full:]], 1)
    return tuple(block[:, i : i + LANES] for i in range(0, full, LANES)) + (tail,)


def packs(rows, width):
    return width > LANES and width % LANES == LANES // 2 and rows % 16 == 0


def packed_shape(rows, width):
    return (rows * width // LANES, LANES) if packs(rows, width) else (rows, width)


def unpack(block, rows, width):
    if not packs(rows, width):
        return block
    full = width - LANES // 2
    count = full // LANES
    pieces = [block[i * rows : (i + 1) * rows] for i in range(count)]
    tail = block[count * rows :]
    pieces.append(jnp.concatenate([tail[:, : LANES // 2], tail[:, LANES // 2 :]], 0))
    return jnp.concatenate(pieces, 1)


def local_kernel(
    seg_total,
    coil_total,
    count_ref,
    time_hbm,
    rows_hbm,
    fourier_hbm,
    cols_hbm,
    field_hbm,
    maps_hbm,
    image_hbm,
    measured_hbm,
    kept_ref,
    away_ref,
    own_ref,
    time_ref,
    rows_ref,
    fourier_ref,
    cols_ref,
    field_ref,
    maps_ref,
    image_ref,
    measured_ref,
    wave_ref,
    phase_ref,
    left_ref,
    right_ref,
    inner_ref,
    misfit_ref,
    row_ref,
    turned_ref,
    factor_ref,
    scaled_ref,
    back_ref,
    term_ref,
    sems,
):
    pixels = field_ref.shape[0]
    row_total = rows_hbm.shape[0]
    col_total = cols_hbm.shape[0]
    own_rows = row_total // seg_total
    width = 2 * pixels // seg_total
    pairs = seg_total // 2
    block_rows = pixels // coil_total
    groups = coil_total // 2
    half = pixels // 2
    cuts = [0] + [half * cut // 192 for cut in CUTS]
    segment = lax.axis_index("seg")
    member = lax.axis_index("coil")

    copies = [
        pltpu.make_async_copy(source, target, sems.at[i])
        for i, (source, target) in enumerate(
            (
                (field_hbm, field_ref),
                (cols_hbm, cols_ref),
                (fourier_hbm, fourier_ref),
                (rows_hbm, rows_ref),
                (time_hbm, time_ref),
                (image_hbm, image_ref),
                (maps_hbm, maps_ref),
                (measured_hbm, measured_ref),
            )
        )
    ]
    for copy in copies:
        copy.start()
    copies[0].wait()

    def phases(first, last):
        for low in range(first, last, PIECE):
            rows = slice(low, low + PIECE)
            sine, cosine = half_angle(field_ref[rows, :])
            twice = 4.0 * (cosine * cosine) - 2.0
            previous = (cosine, -sine)
            for pair in range(pairs):
                if pair == 1:
                    previous, cosine, sine = (
                        (cosine, sine),
                        twice * cosine - cosine,
                        twice * sine + sine,
                    )
                elif pair:
                    previous, cosine, sine = (
                        (cosine, sine),
                        twice * cosine - previous[0],
                        twice * sine - previous[1],
                    )
                phase_ref[2 * pair, rows, :] = cosine
                phase_ref[2 * pair + 1, rows, :] = sine

    first_rows = ZERO * pixels // 384 // PIECE * PIECE
    phases(0, first_rows)
    for copy in copies[1:5]:
        copy.wait()
    early = EARLY * pixels // 384 // PIECE * PIECE
    col_op = dot(cols_ref[...], fourier_ref[...]).astype(jnp.bfloat16)
    phases(first_rows, early)
    left_ref[:col_total, :pixels] = col_op[:, :pixels]
    left_ref[:col_total, pixels:] = -col_op[:, pixels:]
    left_ref[col_total:, :pixels] = col_op[:, pixels:]
    left_ref[col_total:, pixels:] = col_op[:, :pixels]
    col_re = jnp.transpose(col_op[:, :pixels])
    col_im = jnp.transpose(col_op[:, pixels:])
    right_ref[:pixels, :col_total] = col_re
    right_ref[:pixels, col_total:] = col_im
    right_ref[pixels:, :col_total] = -col_im
    right_ref[pixels:, col_total:] = col_re
    row_op = dot(rows_ref[...], fourier_ref[...]).astype(jnp.bfloat16)
    row_ref[...] = row_op

    steps = jnp.broadcast_to(time_ref[...].astype(jnp.float32), (8, row_total))

    def weight(s):
        return jnp.maximum(0.0, 1.0 - jnp.abs(steps - float(s * SUBSTEPS)) / SUBSTEPS)

    along = []
    for pair in range(pairs):
        above, below = weight(pairs + pair), weight(pairs - 1 - pair)
        along += [above + below, above - below]
    for copy in copies[5:]:
        copy.wait()
    for part in range(2):
        adjoint = jnp.transpose(row_op[:, part * pixels : part * pixels + half + LANES])
        if part == 0:
            middle = adjoint[half : half + PIECE].astype(jnp.float32)[:1]
        else:
            top = adjoint[:PIECE].astype(jnp.float32)
            ids = lax.broadcasted_iota(jnp.int32, top.shape, 0)
            top = jnp.where(ids == 0, middle, top).astype(jnp.bfloat16)
            adjoint = jnp.concatenate([top, adjoint[PIECE:half]], 0)
        for i in range(seg_total):
            scaled = adjoint[:half] * along[i][:1].astype(jnp.bfloat16)
            for first, last in zip(cuts, cuts[1:]):
                base = 2 * first * seg_total + (2 * i + part) * (last - first)
                scaled_ref[base : base + last - first, :] = scaled[first:last]

    right = right_ref[...]
    for chunk in range(pixels // CHUNK):
        phases(max(early, chunk * CHUNK), max(early, (chunk + 1) * CHUNK))
        for low in range(0, CHUNK, PIECE):
            rows = slice(chunk * CHUNK + low, chunk * CHUNK + low + PIECE)
            image_re, image_im = image_ref[rows, :pixels], image_ref[rows, pixels:]
            map_re, map_im = maps_ref[rows, :pixels], maps_ref[rows, pixels:]
            base_re = image_re * map_re - image_im * map_im
            base_im = image_re * map_im + image_im * map_re
            for pair in range(pairs):
                cosine = phase_ref[2 * pair, rows, :].astype(jnp.bfloat16)
                sine = phase_ref[2 * pair + 1, rows, :].astype(jnp.bfloat16)
                even = slice(2 * pair * CHUNK + low, 2 * pair * CHUNK + low + PIECE)
                odd = slice(even.start + CHUNK, even.stop + CHUNK)
                wave_ref[chunk, even, :pixels] = base_re * cosine
                wave_ref[chunk, even, pixels:] = base_im * cosine
                wave_ref[chunk, odd, :pixels] = -base_im * sine
                wave_ref[chunk, odd, pixels:] = base_re * sine
        v = dot(wave_ref[chunk], right).astype(jnp.bfloat16)
        for i in range(seg_total):
            piece = v[i * CHUNK : (i + 1) * CHUNK]
            first = slice(chunk * CHUNK, (chunk + 1) * CHUNK)
            second = slice(pixels + first.start, pixels + first.stop)
            lanes = i % 2 * 2 * col_total
            middle, end = lanes + col_total, lanes + 2 * col_total
            inner_ref[i // 2, first, lanes:end] = piece
            inner_ref[i // 2, second, lanes:middle] = -piece[:, col_total:]
            inner_ref[i // 2, second, middle:end] = piece[:, :col_total]
    samples = None
    for pair in range(pairs):
        y = dot(row_ref[...], inner_ref[pair])
        for i in range(2):
            part = y[:, i * 2 * col_total : (i + 1) * 2 * col_total]
            part = part * jnp.transpose(along[2 * pair + i])[:, :1]
            samples = part if samples is None else samples + part

    row_ids = lax.broadcasted_iota(jnp.int32, (row_total, 2 * col_total), 0)
    misfit = samples - measured_ref[...].astype(jnp.float32)
    misfit = jnp.where(row_ids < count_ref[0], misfit, 0.0)
    misfit_ref[...] = misfit
    own_start = pl.multiple_of(segment * own_rows, own_rows)
    own_ref[...] = misfit_ref[pl.ds(own_start, own_rows), :]

    column = lax.rem(segment * width, pixels)
    imaginary = segment * width >= pixels
    start = jnp.minimum(column // LANES * LANES, pixels - WINDOW)
    start = pl.multiple_of(start, LANES)
    after = pl.multiple_of(start + pixels, LANES)
    shift = lax.rem(WINDOW - (column - start), WINDOW)
    misfit = misfit.astype(jnp.bfloat16)
    turn_re = dot(misfit, left_ref[:, pl.ds(start, WINDOW)]).astype(jnp.bfloat16)
    turn_im = dot(misfit, left_ref[:, pl.ds(after, WINDOW)]).astype(jnp.bfloat16)
    turned_ref[:, :WINDOW] = turn_re
    turned_ref[:, WINDOW:] = turn_im
    turned = turned_ref[...]
    factor = coil_total ** (-0.5)
    for low in range(0, pixels, PIECE):
        rows = slice(low, low + PIECE)
        map_re = maps_ref[rows, pl.ds(start, WINDOW)].astype(jnp.float32)
        map_im = maps_ref[rows, pl.ds(after, WINDOW)].astype(jnp.float32)
        factor_ref[0, rows, :] = jnp.where(imaginary, -map_im, map_re) * factor
        factor_ref[1, rows, :] = jnp.where(imaginary, map_re, map_im) * factor
    ids = lax.broadcasted_iota(jnp.int32, (PIECE, WINDOW), 0)

    def mirrored(ref, k, low, lanes):
        if low:
            return reverse_rows(ref[k, pixels - low - PIECE + 1 : pixels - low + 1, lanes])
        block = pltpu.roll(reverse_rows(ref[k, pixels - PIECE : pixels, lanes]), 1, 0)
        return jnp.where(ids == 0, ref[k, half : half + 8, lanes][:1], block)

    for first, last in zip(cuts, cuts[1:]):
        tall = last - first
        part = slice(2 * first * seg_total, 2 * last * seg_total)
        back_ref[part, :] = dot(scaled_ref[part, :], turned)
        for low in range(first, last, PIECE):
            rows = slice(low, low + PIECE)
            lanes = pl.ds(start, WINDOW)
            sums = None
            for pair in range(pairs):
                images = []
                for i in (2 * pair, 2 * pair + 1):
                    base = 2 * first * seg_total + 2 * i * tall + low - first
                    real = [back_ref[base : base + PIECE, at : at + WINDOW] for at in (0, WINDOW)]
                    base += tall
                    turn = [back_ref[base : base + PIECE, at : at + WINDOW] for at in (0, WINDOW)]
                    other = real
                    if low == 0:
                        other = [jnp.where(ids == 0, q, p) for p, q in zip(real, turn)]
                        turn = [jnp.where(ids == 0, 0.0, q) for q in turn]
                    images.append(
                        (
                            real[0] + turn[1],
                            real[1] - turn[0],
                            other[0] - turn[1],
                            other[1] + turn[0],
                        )
                    )
                even, odd = images
                cosine = phase_ref[2 * pair, rows, lanes]
                sine = phase_ref[2 * pair + 1, rows, lanes]
                cosine_far = mirrored(phase_ref, 2 * pair, low, lanes)
                sine_far = mirrored(phase_ref, 2 * pair + 1, low, lanes)
                adds = [
                    cosine * even[0] + sine * odd[1],
                    cosine * even[1] - sine * odd[0],
                    cosine_far * even[2] + sine_far * odd[3],
                    cosine_far * even[3] - sine_far * odd[2],
                ]
                sums = adds if sums is None else [x + y for x, y in zip(sums, adds)]
            near = factor_ref[0, rows, :] * sums[0] + factor_ref[1, rows, :] * sums[1]
            everything = slice(None)
            far = mirrored(factor_ref, 0, low, everything) * sums[2]
            far = far + mirrored(factor_ref, 1, low, everything) * sums[3]
            term_ref[rows, :] = pltpu.roll(near, shift, 1)
            far = reverse_rows(pltpu.roll(far, shift, 1))
            top = pixels - low - PIECE + 1
            if low:
                term_ref[top : top + PIECE, :] = far
            else:
                term_ref[top:pixels, :] = far[: PIECE - 1]
                term_ref[half : half + 1, :] = far[PIECE - 1 :]

    lane = lax.rem(member, 2)
    group = member // 2
    for g in range(groups):
        slot = slot_of(g, group, groups)
        upper = term_ref[2 * g * block_rows : (2 * g + 1) * block_rows, :width]
        lower = term_ref[(2 * g + 1) * block_rows : (2 * g + 2) * block_rows, :width]
        for ref, value in (
            (kept_ref, jnp.where(lane == 0, upper, lower)),
            (away_ref, jnp.where(lane == 0, lower, upper)),
        ):
            top = 0
            for piece in pack(value):
                ref[slot, top : top + piece.shape[0], :] = piece
                top += piece.shape[0]


def local_terms(seg_total, coil_total, image, maps, field, rows, cols, measured, time, count):
    pixels = field.shape[0]
    row_total, col_total = rows.shape[0], cols.shape[0]
    width = 2 * pixels // seg_total
    fourier = jnp.asarray(dft_tables(pixels), jnp.bfloat16)
    anywhere = pl.BlockSpec(memory_space=pl.ANY)
    vmem = pl.BlockSpec(memory_space=pltpu.VMEM)
    smem = pl.BlockSpec(memory_space=pltpu.SMEM)
    operands = (time, rows, fourier, cols, field, maps, image, measured)
    blocks = (coil_total // 2, *packed_shape(pixels // coil_total, width))
    return pl.pallas_call(
        functools.partial(local_kernel, seg_total, coil_total),
        out_shape=(
            pltpu.VMEM(blocks, jnp.float32),
            pltpu.VMEM(blocks, jnp.float32),
            pltpu.VMEM((row_total // seg_total, 2 * col_total), jnp.float32),
        ),
        in_specs=[smem] + [anywhere] * len(operands),
        out_specs=(vmem, vmem, vmem),
        scratch_shapes=[pltpu.VMEM(x.shape, x.dtype) for x in operands]
        + [
            pltpu.VMEM((pixels // CHUNK, seg_total * CHUNK, 2 * pixels), jnp.bfloat16),
            pltpu.VMEM((seg_total, pixels, pixels), jnp.float32),
            pltpu.VMEM((2 * col_total, 2 * pixels), jnp.bfloat16),
            pltpu.VMEM((2 * pixels, 2 * col_total), jnp.bfloat16),
            pltpu.VMEM((seg_total // 2, 2 * pixels, 4 * col_total), jnp.bfloat16),
            pltpu.VMEM((row_total, 2 * col_total), jnp.float32),
            pltpu.VMEM((row_total, 2 * pixels), jnp.bfloat16),
            pltpu.VMEM((row_total, 2 * WINDOW), jnp.bfloat16),
            pltpu.VMEM((2, pixels, WINDOW), jnp.float32),
            pltpu.VMEM((seg_total * pixels, row_total), jnp.bfloat16),
            pltpu.VMEM((seg_total * pixels, 2 * WINDOW), jnp.float32),
            pltpu.VMEM((pixels, WINDOW), jnp.float32),
            pltpu.SemaphoreType.DMA((8,)),
        ],
        compiler_params=pltpu.CompilerParams(vmem_limit_bytes=56 * 1024 * 1024),
        name="local_terms",
    )(count, *operands)


def routes(groups):
    if groups == 4:
        return [(2, 0, 3, 1), (1, 3, 0, 2), (3, 2, 1, 0)]
    return [tuple((z + step) % groups for z in range(groups)) for step in range(1, groups)]


def slot_of(target, group, groups):
    slot = jnp.int32(groups - 1)
    if groups != 4:
        return lax.rem(target + 2 * groups - 1 - group, groups)
    for k, route in enumerate(routes(groups)):
        slot = jnp.where(group == route.index(target), k, slot)
    return slot


def exchange_sum(kept, away, axis):
    total = lax.axis_size(axis)
    last = total // 2 - 1
    swap = [(i, i ^ 1) for i in range(total)]
    plan = [[(i, 2 * route[i // 2] + i % 2) for i in range(total)] for route in routes(total // 2)]
    got = lax.ppermute(away[1:last], axis, swap)
    both = lax.ppermute(jnp.stack([kept[0], away[0]]), axis, plan[0])
    paired = kept[1:last] + got
    result = kept[last] + both[0]
    for k in range(1, last):
        got = lax.ppermute(paired[k - 1], axis, plan[k])
        result = result + got
    got = lax.ppermute(away[last] + both[1], axis, swap)
    return result + got


def shards(
    image_estimate,
    coil_maps,
    field_map,
    interp_rows,
    interp_cols,
    measured,
    sample_time,
    sample_count,
):
    seg_total = lax.axis_size("seg")
    coil_total = lax.axis_size("coil")
    pixels = field_map.shape[0]
    kept, away, own = local_terms(
        seg_total,
        coil_total,
        image_estimate[0],
        coil_maps[0],
        field_map,
        interp_rows[0],
        interp_cols[0],
        measured[0, 0],
        sample_time,
        sample_count,
    )
    total = exchange_sum(kept, away, "coil")
    gradient = unpack(total, pixels // coil_total, 2 * pixels // seg_total)
    return gradient[None], own[None, None]


def solution(mesh):
    in_specs = (P(), P("coil", None, None), P(), P(), P(), P("coil", None, None, None), P(), P())
    out_specs = (P(None, "coil", "seg"), P("coil", None, "seg", None))
    return jax.shard_map(
        shards, mesh=mesh, in_specs=in_specs, out_specs=out_specs, check_vma=False
    )
```
